512 devices in a mesh: leaf: 64 (over y, z_lo, core), grp: 8 (over z_hi, x).
Axes of the slice: x: 4, y: 4, z: 16 (z_hi: 2, z_lo: 8; z = z_hi * 8 + z_lo), core: 2. Of those that a mesh axis runs over, the one named last changes fastest.
Arguments:
- slot_parent: int32 [512], P(('leaf', 'grp')), may hold values from -1 to 7, as said below
- leaf_matrix: float32 [512, 384, 384], P(('leaf', 'grp')), as said below
- coupling: float32 [512, 384, 128], P(('leaf', 'grp')), may hold values from -0.3125 to 0.3125
- leaf_residual_rows: float32 [512, 384], P(('leaf', 'grp')), may hold values from -6 to 6
- node_matrix: float32 [64, 128, 128], P('grp', 'leaf'), as said below
- node_link: float32 [64, 128, 128], P('grp', 'leaf'), may hold values from -0.5 to 0.5
- node_rhs: float32 [64, 128], P('grp', 'leaf'), may hold values from -6 to 6
- root_matrix: float32 [128, 128], replicated, as said below
- root_rhs: float32 [128], replicated, may hold values from -6 to 6
Outputs:
- leaf_dir: float32 [512, 384], P(('leaf', 'grp'))
- node_dir: float32 [64, 128], P('grp', 'leaf')
- root_dir: float32 [128], replicated
The draws below stay inside these ranges and needn't reach their ends.
Inputs may be any that keep to these rules, and one draw needn't show every extreme that they name: `slot_parent`: -1 marks an empty slot; otherwise the value is the section-2 node, among the 8 nodes of the slot's grp index, to which the leaf belongs. On every device the live slots come first; a device may hold no live slot or only live slots. `leaf_matrix`: each block is symmetric positive definite with smallest eigenvalue at least 0.1. `node_matrix`: each block is symmetric positive definite with smallest eigenvalue at least 0.1. `root_matrix`: symmetric positive definite with smallest eigenvalue at least 0.1.
All inputs are finite; a program needn't handle non-finite values.
Results may differ from the reference program's by a relative error of at most 0.00018.
Values sent between devices are 32-bit elements; how exact they have to be, the bound alone decides.
A program may use at most 64 MiB of HBM per device.

```python
import math
import jax
import jax.numpy as jnp
from jax import lax

LEAF_ROWS = 384
LINK_WIDTH = 128
R = 128
GROUP_NODES = 8
DEVICE_SLOTS = 1
TOTAL_SLOTS = 512
NODES = 64
N_GRP = 8


def positive_definite_blocks(base_key, block_count, matrix_order):
    block_keys = jax.random.split(base_key, block_count)

    def one_block(block_key):
        entry_key, margin_key = jax.random.split(block_key)
        factor = jax.random.normal(entry_key, (matrix_order, matrix_order), jnp.float32)
        margin = jnp.exp(jax.random.uniform(margin_key, (matrix_order,), jnp.float32, math.log(0.1), math.log(3.0)))
        product = jnp.dot(factor, factor.T, precision=lax.Precision.HIGHEST)
        product = (product + product.T) * (0.5 / matrix_order)
        identity = jnp.eye(matrix_order, dtype=jnp.float32)
        return product + identity * margin[:, None]
    return lax.map(one_block, block_keys)


def draw_leaf_matrix(key, part):
    return positive_definite_blocks(jax.random.fold_in(key, 11), TOTAL_SLOTS, LEAF_ROWS)


def draw_node_matrix(key, part):
    return positive_definite_blocks(jax.random.fold_in(key, 12), NODES, LINK_WIDTH)


def draw_root_matrix(key, part):
    return positive_definite_blocks(jax.random.fold_in(key, 13), 1, R)[0]


def draw_slot_parent(key, part):
    base_key = jax.random.fold_in(key, 14)
    count_key, parent_random_key = jax.random.split(base_key)
    device_list = TOTAL_SLOTS // DEVICE_SLOTS
    active_count = jax.random.randint(count_key, (device_list,), 0, DEVICE_SLOTS + 1)
    active_count = active_count.at[0].set(0).at[device_list - 1].set(DEVICE_SLOTS)
    parent_nodes = jax.random.randint(parent_random_key, (TOTAL_SLOTS,), 0, GROUP_NODES)
    parent_nodes = parent_nodes.at[TOTAL_SLOTS - 1].set(GROUP_NODES - 1)
    slot_position = jnp.arange(TOTAL_SLOTS, dtype=jnp.int32) % DEVICE_SLOTS
    owning_index = jnp.arange(TOTAL_SLOTS, dtype=jnp.int32) // DEVICE_SLOTS
    return jnp.where(slot_position < active_count[owning_index], parent_nodes, -1).astype(jnp.int32)


def levels(key, dims, cuts, low, largest):
    gain = 1.0
    for dim, parts in cuts:
        heights = jax.random.uniform(jax.random.fold_in(jax.random.fold_in(key, 6), dim), (parts,), jnp.float32, low / len(cuts), largest / len(cuts))
        gain = gain * jnp.repeat(jnp.exp(heights), dims[dim] // parts).reshape((-1,) + (1,) * (len(dims) - 1 - dim))
    return gain


def noise(key, extent, scale, limit, pieces=(), kind=jnp.bfloat16):
    drawn = scale * jax.random.normal(key, extent, jnp.float32)
    if pieces:
        drawn = drawn * levels(key, extent, pieces, -0.22, 0.18)
    return jnp.clip(drawn, -limit, limit).astype(kind)


def setup_inputs(seed: int = 0) -> dict:
    seeds = jax.random.split(jax.random.key(seed), 10)
    return {
        "slot_parent": draw_slot_parent(jax.random.fold_in(seeds[9], 71), 0),
        "leaf_matrix": draw_leaf_matrix(jax.random.fold_in(seeds[9], 71), 0),
        "coupling": noise(seeds[2], (TOTAL_SLOTS, LEAF_ROWS, LINK_WIDTH), LEAF_ROWS ** -0.5, 0.3125, ((0, 512),), jnp.float32),
        "leaf_residual_rows": noise(seeds[3], (TOTAL_SLOTS, LEAF_ROWS), 1.0, 6.0, ((0, 512),), jnp.float32),
        "node_matrix": draw_node_matrix(jax.random.fold_in(seeds[9], 71), 0),
        "node_link": noise(seeds[5], (NODES, LINK_WIDTH, R), LINK_WIDTH ** -0.5, 0.5, ((0, 8), (1, 64)), jnp.float32),
        "node_rhs": noise(seeds[6], (NODES, LINK_WIDTH), 1.0, 6.0, ((0, 8), (1, 64)), jnp.float32),
        "root_matrix": draw_root_matrix(jax.random.fold_in(seeds[9], 71), 0),
        "root_rhs": noise(seeds[8], (R,), 1.0, 6.0, (), jnp.float32),
    }


highest = lax.Precision.HIGHEST

def lower_solve(factor, values):
    return lax.linalg.triangular_solve(factor, values, left_side=True, lower=True)

def upper_solve(factor, values):
    return lax.linalg.triangular_solve(factor, values, left_side=True, lower=True, transpose_a=True)

def leaf_factor(matrix, cpl_block, rhs_block):
    factor = jnp.linalg.cholesky(matrix)
    solved = lower_solve(factor, cpl_block)
    reduced = lower_solve(factor, rhs_block[:, None])[:, 0]
    return (factor, solved, reduced)

def reference(slot_parent, leaf_matrix, coupling, leaf_residual_rows, node_matrix, node_link, node_rhs, root_matrix, root_rhs):
    slot_numbers = jnp.arange(TOTAL_SLOTS, dtype=jnp.int32)
    set_index = slot_numbers // DEVICE_SLOTS % N_GRP
    active = slot_parent >= 0
    target = jnp.where(active, set_index * GROUP_NODES + slot_parent, 0).astype(jnp.int32)
    weight = active.astype(jnp.float32)

    def accumulate(carry, item):
        matrix, cpl_block, rhs_block, node_index, live_weight = item
        factor, solved, reduced = leaf_factor(matrix, cpl_block, rhs_block)
        gram = jnp.dot(solved.T, solved, precision=highest)
        projected = jnp.dot(solved.T, reduced, precision=highest)
        sums, vectors = carry
        sums = sums.at[node_index].add(live_weight * gram)
        vectors = vectors.at[node_index].add(live_weight * projected)
        return ((sums, vectors), None)
    start = (jnp.zeros((NODES, LINK_WIDTH, LINK_WIDTH), jnp.float32), jnp.zeros((NODES, LINK_WIDTH), jnp.float32))
    (sums, vectors), unused = lax.scan(accumulate, start, (leaf_matrix, coupling, leaf_residual_rows, target, weight))
    schur = node_matrix + sums
    node_vec = vectors - node_rhs
    node_fac = jnp.linalg.cholesky(schur)
    link_solved = lower_solve(node_fac, node_link)
    vec_solved = lower_solve(node_fac, node_vec[:, :, None])[:, :, 0]
    root_sys = root_matrix + jnp.einsum('kar,kas->rs', link_solved, link_solved, precision=highest)
    root_vec = root_rhs - jnp.einsum('kar,ka->r', link_solved, vec_solved, precision=highest)
    root_fac = jnp.linalg.cholesky(root_sys)
    root_dir = upper_solve(root_fac, lower_solve(root_fac, root_vec[:, None]))[:, 0]
    moved = vec_solved + jnp.einsum('kar,r->ka', link_solved, root_dir, precision=highest)
    node_dir = upper_solve(node_fac, moved[:, :, None])[:, :, 0]

    def leaf_solve(item):
        matrix, cpl_block, rhs_block, node_index, live_weight = item
        factor, solved, reduced = leaf_factor(matrix, cpl_block, rhs_block)
        parent_dir = node_dir[node_index]
        correction = reduced - jnp.dot(solved, parent_dir, precision=highest)
        return live_weight * upper_solve(factor, correction[:, None])[:, 0]
    leaf_dir = lax.map(leaf_solve, (leaf_matrix, coupling, leaf_residual_rows, target, weight))
    return (leaf_dir, node_dir, root_dir)
```

```python
import jax
import jax.numpy as jnp
from jax import lax
from jax.experimental import pallas as pl
from jax.experimental.pallas import tpu as pltpu
from jax.sharding import PartitionSpec as P

f32 = jnp.float32
MESH = pl.DeviceIdType.MESH
HI = lax.Precision.HIGHEST
N = 128
AUG = 136


def dot(a, b):
    return jnp.dot(a, b, precision=HI, preferred_element_type=f32)


def dot_nt(a, b):
    return lax.dot_general(
        a, b, (((1,), (1,)), ((), ())), precision=HI, preferred_element_type=f32
    )


def lane_bcast(x, index):
    return jnp.take_along_axis(x, index, axis=1, mode="promise_in_bounds")


def row_bcast(row):
    return jnp.broadcast_to(row, (8, N))


def invert(d_ref, p_ref):
    lane = lax.broadcasted_iota(jnp.int32, (8, N), 1)
    sub = lax.broadcasted_iota(jnp.int32, (8, N), 0)
    groups = N // 8
    first = d_ref[0:8, :]
    for j in range(8):
        p_ref[8 * j : 8 * j + 8, :] = lane_bcast(first, jnp.full((8, N), j, jnp.int32))

    def block(k, carry):
        base = pl.multiple_of(k * 8, 8)
        base_next = pl.multiple_of(jnp.minimum(k + 1, groups - 1) * 8, 8)
        here = [jnp.full((8, N), base + j, jnp.int32) for j in range(8)]
        after = [jnp.full((8, N), base_next + j, jnp.int32) for j in range(8)]
        s = {}
        for j in range(8):
            for i in range(j + 1):
                s[i, j] = row_bcast(p_ref[8 * j + i : 8 * j + i + 1, :])
        r = [row_bcast(d_ref[pl.ds(base + j, 1), :]) for j in range(8)]
        d = [d_ref[g * 8 : (g + 1) * 8, :] for g in range(groups)]
        dn = d_ref[pl.ds(base_next, 8), :]
        c, cn = [], []
        for j in range(8):
            cn.append(lane_bcast(dn, here[j]))
            c.append([lane_bcast(d[g], here[j]) for g in range(groups)])
        inside = (lane >= base) & (lane < base + 8)
        r = [jnp.where(inside, jnp.where(lane == base + j, 1.0, 0.0), r[j]) for j in range(8)]
        low, inv = {}, []
        for j in range(8):
            inv.append(1.0 / s[j, j])
            for i in range(j + 1, 8):
                low[i, j] = s[j, i] * inv[j]
            for i in range(j + 1, 8):
                for m in range(i, 8):
                    s[i, m] = s[i, m] - low[i, j] * s[j, m]
            for i in range(j + 1, 8):
                r[i] = r[i] - low[i, j] * r[j]
        x = [r[j] * inv[j] for j in range(8)]
        for j in range(7, -1, -1):
            for i in range(j):
                x[i] = x[i] - low[j, i] * x[j]

        def update(rows, cols):
            kept = jnp.where(inside, 0.0, rows)
            t = [cols[j] * x[j] for j in range(8)]
            return kept - (((t[0] + t[1]) + (t[2] + t[3])) + ((t[4] + t[5]) + (t[6] + t[7])))

        upcoming = update(dn, cn)
        for j in range(8):
            p_ref[8 * j : 8 * j + 8, :] = lane_bcast(upcoming, after[j])
        for g in range(groups):
            d_ref[g * 8 : (g + 1) * 8, :] = update(d[g], [c[j][g] for j in range(8)])
        new = x[0]
        for j in range(1, 8):
            new = jnp.where(sub == j, x[j], new)
        d_ref[pl.ds(base, 8), :] = new
        return carry

    lax.fori_loop(0, groups, block, 0)


def kernel(
    parent, amat, coup, resid, nmat, nlink, nrhs, rmat, rrhs,
    leaf_out, node_out, root_out,
    bt, dinv, pbuf, e1, rem1, e2, rem2, h3, wts,
    ntile, gath, snd, recv_y, acc_o, recv_c, acc_m, recv_z,
    nsys, nlinks, naug, hmat, rparts, send_r, recv_r, part, recv_g, tot, recv_t,
    msg, recv_n, zt, nd8,
    s_n, r_n, s_y, r_y, s_c, r_c, s_z, r_z, s_r, r_r, s_g, r_g, s_t, r_t, s_m, r_m,
):
    me = lax.axis_index("leaf")
    grp = lax.axis_index("grp")
    y, z, core = me // 16, (me // 2) % 8, me % 2
    own_z = 4 - grp // 4
    owner = z == own_z
    mine = 2 * y + core

    def dev(leaf):
        return {"leaf": leaf, "grp": grp}

    def owner_leaf(m, oz):
        return (m // 2) * 16 + oz * 2 + m % 2

    barrier = pltpu.get_barrier_semaphore()

    def greet(t, carry):
        pl.semaphore_signal(barrier, inc=1, device_id=dev((me + t) % 64), device_id_type=MESH)
        return carry

    lax.fori_loop(1, 64, greet, 0)

    @pl.when(owner)
    def _():
        def greet_far(t, carry):
            g = (grp + t) % 8
            pl.semaphore_signal(
                barrier, inc=1,
                device_id={"leaf": owner_leaf(mine, 4 - g // 4), "grp": g}, device_id_type=MESH,
            )
            return carry

        lax.fori_loop(1, 8, greet_far, 0)

    sub = lax.broadcasted_iota(jnp.int32, (8, N), 0)
    lane = lax.broadcasted_iota(jnp.int32, (8, N), 1)
    wts[...] = jnp.where(sub == parent[0], 1.0, 0.0)
    for b in range(3):
        bt[0:N, b * N : (b + 1) * N] = coup[0, b * N : (b + 1) * N, :].T
        bt[N:AUG, b * N : (b + 1) * N] = jnp.where(
            sub == 0, row_bcast(resid[:, b * N : (b + 1) * N]), 0.0
        )
    nd8[...] = jnp.zeros((8, N), f32)
    nd8[:, 0:2] = nrhs[...]
    shifted = pltpu.roll(nd8[...], 2 * me, 1)
    for q in range(8):
        ntile[q, 0:2, :] = nmat[q]
        ntile[q, 2:4, :] = nlink[q]
        ntile[q, 4:8, :] = jnp.where(
            lax.broadcasted_iota(jnp.int32, (4, N), 0) == 0,
            jnp.broadcast_to(shifted[q : q + 1, :], (4, N)), 0.0
        )

    dinv[...] = amat[0, 0:N, 0:N]
    invert(dinv, pbuf)

    @pl.when(owner)
    def _():
        pl.semaphore_wait(barrier, 70)

    @pl.when(jnp.logical_not(owner))
    def _():
        pl.semaphore_wait(barrier, 63)

    def node_copy(q, target):
        return pltpu.make_async_remote_copy(
            src_ref=ntile.at[q], dst_ref=gath.at[me], send_sem=s_n.at[q], recv_sem=r_n,
            device_id=dev(target), device_id_type=MESH,
        )

    for q in range(8):
        target = owner_leaf(q, own_z)

        @pl.when(target != me)
        def _():
            node_copy(q, target).start()

        @pl.when(target == me)
        def _():
            gath[me] = ntile[q]

    d1 = dinv[...]
    e1[0:256, :] = dot(amat[0, N:384, 0:N], d1)
    e1[256:392, :] = dot(bt[:, 0:N], d1)
    snd[0:AUG, :] = dot_nt(e1[256:392, :], bt[0:N, 0:N])
    rem1[0:256, :] = amat[0, N:384, N:384] - dot(e1[0:256, :], amat[0, 0:N, N:384])
    rem1[256:392, :] = bt[:, N:384] - dot(e1[256:392, :], amat[0, 0:N, N:384])
    dinv[...] = rem1[0:N, 0:N]
    invert(dinv, pbuf)
    e2[...] = dot(rem1[N:392, 0:N], dinv[...])
    snd[0:AUG, :] += dot_nt(e2[N:264, :], rem1[256:384, 0:N])
    rem2[...] = rem1[N:392, N:256] - dot(e2[...], rem1[0:N, N:256])
    dinv[...] = rem2[0:N, :]
    invert(dinv, pbuf)
    h3[...] = dot(rem2[N:264, :], dinv[...])
    snd[0:AUG, :] += dot_nt(h3[...], rem2[N:256, :])
    snd[AUG : AUG + 8, :] = wts[...]

    def y_copy(t):
        return pltpu.make_async_remote_copy(
            src_ref=snd, dst_ref=recv_y.at[t - 1], send_sem=s_y.at[t - 1], recv_sem=r_y.at[t - 1],
            device_id=dev(((y + t) % 4) * 16 + z * 2 + core), device_id_type=MESH,
        )

    for t in (1, 2, 3):
        y_copy(t).start()
    other = 2 * y + 1 - core
    acc_m[...] = snd[0:AUG, :] * snd[pl.ds(AUG + mine, 1), :]
    acc_o[...] = snd[0:AUG, :] * snd[pl.ds(AUG + other, 1), :]
    for t in (1, 3, 2):
        y_copy(t).wait_recv()
        acc_m[...] += recv_y[t - 1, 0:AUG, :] * recv_y[t - 1, pl.ds(AUG + mine, 1), :]
        acc_o[...] += recv_y[t - 1, 0:AUG, :] * recv_y[t - 1, pl.ds(AUG + other, 1), :]
    core_copy = pltpu.make_async_remote_copy(
        src_ref=acc_o, dst_ref=recv_c, send_sem=s_c, recv_sem=r_c,
        device_id=dev(me + 1 - 2 * core), device_id_type=MESH,
    )
    core_copy.start()
    core_copy.wait_recv()
    acc_m[...] += recv_c[...]

    def z_copy(source):
        return pltpu.make_async_remote_copy(
            src_ref=acc_m, dst_ref=recv_z.at[source], send_sem=s_z, recv_sem=r_z.at[source],
            device_id=dev(owner_leaf(mine, own_z)), device_id_type=MESH,
        )

    @pl.when(jnp.logical_not(owner))
    def _():
        z_copy(z).start()

    def slice_copy(src, dst, send_sem, recv_sem, t, by_group):
        if by_group:
            target = (grp + t) % 8
            device = {"leaf": owner_leaf(mine, 4 - target // 4), "grp": target}
            slot = grp
            source = src
        else:
            target = (mine + t) % 8
            device = dev(owner_leaf(target, own_z))
            slot = mine
            source = src
        return pltpu.make_async_remote_copy(
            src_ref=source, dst_ref=dst.at[slot], send_sem=send_sem.at[t], recv_sem=recv_sem.at[slot],
            device_id=device, device_id_type=MESH,
        )

    def slot_wait(dst, send_sem, recv_sem, slot):
        pltpu.make_async_remote_copy(
            src_ref=dst.at[slot], dst_ref=dst.at[slot], send_sem=send_sem.at[0],
            recv_sem=recv_sem.at[slot], device_id=dev(me + 1 - 2 * core), device_id_type=MESH,
        ).wait_recv()

    def message(t):
        return pltpu.make_async_remote_copy(
            src_ref=msg, dst_ref=recv_n.at[mine], send_sem=s_m.at[t], recv_sem=r_m.at[mine],
            device_id=dev((me + t) % 64), device_id_type=MESH,
        )

    @pl.when(owner)
    def _():
        pltpu.make_async_remote_copy(
            src_ref=gath.at[pl.ds(0, 63)], dst_ref=gath.at[pl.ds(0, 63)], send_sem=s_n.at[0],
            recv_sem=r_n, device_id=dev(me + 1 - 2 * core), device_id_type=MESH,
        ).wait_recv()
        rhs = jnp.zeros((4, N), f32)
        for i in range(64):
            tile = gath[i]
            nsys[2 * i : 2 * i + 2, :] = tile[0:2, :]
            nlinks[2 * i : 2 * i + 2, :] = tile[2:4, :]
            rhs = rhs + tile[4:8, :]
        naug[0:N, :] = nlinks[...].T
        acc_m[N : N + 4, :] += -rhs
        acc_m[0:N, :] += nsys[...]
        for t in (1, 7, 2, 6, 3, 5, 4):
            source = (own_z + t) % 8
            z_copy(source).wait_recv()
            acc_m[...] += recv_z[source]
        dinv[...] = acc_m[0:N, :]
        naug[N:AUG, :] = acc_m[N:AUG, :]
        invert(dinv, pbuf)
        hmat[...] = dot(naug[...], dinv[...])
        rparts[...] = dot(hmat[...], nlinks[...])
        for q in range(8):
            send_r[q, 0:16, :] = rparts[16 * q : 16 * q + 16, :]
            send_r[q, 16:24, :] = rparts[N:AUG, :]

        for t in range(1, 8):
            slice_copy(send_r.at[(mine + t) % 8], recv_r, s_r, r_r, t, False).start()
        recv_r[mine] = send_r[mine]
        for t in range(1, 8):
            slot_wait(recv_r, s_r, r_r, (mine + t) % 8)
        total = recv_r[0]
        for q in range(1, 8):
            total = total + recv_r[q]
        part[...] = total
        for t in range(1, 8):
            slice_copy(part, recv_g, s_g, r_g, t, True).start()
        recv_g[grp] = total
        for t in range(1, 8):
            slot_wait(recv_g, s_g, r_g, (grp + t) % 8)
        total = recv_g[0]
        for q in range(1, 8):
            total = total + recv_g[q]
        tot[...] = total
        for t in range(1, 8):
            slice_copy(tot, recv_t, s_t, r_t, t, False).start()
        recv_t[mine] = total
        for t in range(1, 8):
            slot_wait(recv_t, s_t, r_t, (mine + t) % 8)
        for q in range(8):
            dinv[16 * q : 16 * q + 16, :] = rmat[16 * q : 16 * q + 16, :] + recv_t[q, 0:16, :]
        invert(dinv, pbuf)
        root_vec = row_bcast(rrhs[...]) - row_bcast(total[16:17, :])
        root = dot(root_vec, dinv[...])
        node = row_bcast(hmat[N : N + 1, :]) + dot(root, hmat[0:N, :])
        msg[0:1, :] = node[0:1, :]
        msg[1:2, :] = root[0:1, :]

        def send(t, carry):
            message(t).start()
            return carry

        lax.fori_loop(1, 64, send, 0)
        recv_n[mine] = msg[...]

    zt[:, 256:384] = h3[...]
    zt[:, N:256] = e2[N:264, :] - dot(h3[...], e2[0:N, :])
    zt[:, 0:N] = e1[256:392, :] - dot(zt[:, N:384], e1[0:256, :])

    for q in range(8):
        @pl.when(jnp.logical_or(jnp.logical_not(owner), mine != q))
        def _():
            slot_wait(recv_n, s_m, r_m, q)

    parent_dir = jnp.zeros((8, N), f32)
    for q in range(8):
        direction = row_bcast(recv_n[q, 0:1, :])
        parent_dir = parent_dir + direction * row_bcast(wts[q : q + 1, :])
        nd8[q : q + 1, :] = recv_n[q, 0:1, :]
    live = jnp.sum(wts[...], axis=0, keepdims=True)
    moved = dot(parent_dir, zt[0:N, :])
    for b in range(3):
        cols = slice(b * N, (b + 1) * N)
        leaf_out[:, cols] = (zt[N : N + 1, cols] - moved[0:1, cols]) * live
    node_out[...] = pltpu.roll(nd8[...], (N - 2 * me) % N, 1)[:, 0:2]
    root_out[...] = recv_n[0, 1:2, :]

    for q in range(8):
        target = owner_leaf(q, own_z)

        @pl.when(target != me)
        def _():
            node_copy(q, target).wait_send()

    for t in (1, 2, 3):
        y_copy(t).wait_send()
    core_copy.wait_send()

    @pl.when(jnp.logical_not(owner))
    def _():
        z_copy(z).wait_send()

    @pl.when(owner)
    def _():
        for t in range(1, 8):
            slice_copy(send_r.at[(mine + t) % 8], recv_r, s_r, r_r, t, False).wait_send()
            slice_copy(part, recv_g, s_g, r_g, t, True).wait_send()
            slice_copy(tot, recv_t, s_t, r_t, t, False).wait_send()

        def drain(t, carry):
            message(t).wait_send()
            return carry

        lax.fori_loop(1, 64, drain, 0)


def body(
    slot_parent, leaf_matrix, coupling, leaf_residual_rows, node_matrix, node_link, node_rhs,
    root_matrix, root_rhs,
):
    vmem = pl.BlockSpec(memory_space=pltpu.VMEM)
    buf = lambda *shape: pltpu.VMEM(shape, f32)
    dma = pltpu.SemaphoreType.DMA
    leaf_dir, node_dir, root_dir = pl.pallas_call(
        kernel,
        out_shape=(
            jax.ShapeDtypeStruct((1, 384), f32),
            jax.ShapeDtypeStruct((8, 2), f32),
            jax.ShapeDtypeStruct((1, N), f32),
        ),
        in_specs=[pl.BlockSpec(memory_space=pltpu.SMEM)] + [vmem] * 8,
        out_specs=(vmem, vmem, vmem),
        scratch_shapes=[
            buf(AUG, 384), buf(N, N), buf(64, N), buf(392, N), buf(392, 256), buf(264, N),
            buf(264, N), buf(AUG, N), buf(8, N),
            buf(8, 8, N), buf(64, 8, N), buf(144, N), buf(3, 144, N), buf(AUG, N), buf(AUG, N),
            buf(AUG, N), buf(8, AUG, N),
            buf(N, N), buf(N, N), buf(AUG, N), buf(AUG, N), buf(AUG, N), buf(8, 24, N),
            buf(8, 24, N), buf(24, N), buf(8, 24, N), buf(24, N), buf(8, 24, N),
            buf(2, N), buf(8, 2, N), buf(AUG, 384), buf(8, N),
            dma((8,)), dma, dma((3,)), dma((3,)), dma, dma, dma, dma((8,)),
            dma((8,)), dma((8,)), dma((8,)), dma((8,)), dma((8,)), dma((8,)), dma((64,)), dma((8,)),
        ],
        compiler_params=pltpu.CompilerParams(collective_id=0, has_side_effects=True),
        name="newton_step",
    )(
        slot_parent, leaf_matrix, coupling, leaf_residual_rows, node_matrix, node_link, node_rhs,
        root_matrix, root_rhs[None, :],
    )
    return leaf_dir, node_dir, root_dir[0]


def solution(mesh):
    return jax.shard_map(
        body,
        mesh=mesh,
        in_specs=(
            P(("leaf", "grp")),
            P(("leaf", "grp"), None, None),
            P(("leaf", "grp"), None, None),
            P(("leaf", "grp"), None),
            P("grp", "leaf", None),
            P("grp", "leaf", None),
            P("grp", "leaf"),
            P(),
            P(),
        ),
        out_specs=(P(("leaf", "grp"), None), P("grp", "leaf"), P()),
        check_vma=False,
    )
```

```python
import jax
import jax.numpy as jnp
from jax import lax
from jax.experimental import pallas as pl
from jax.experimental.pallas import tpu as pltpu
from jax.sharding import PartitionSpec as P

f32 = jnp.float32
MESH = pl.DeviceIdType.MESH
HI = lax.Precision.HIGHEST
N = 128
AUG = 136


def dot(a, b):
    return jnp.dot(a, b, precision=HI, preferred_element_type=f32)


def dot_nt(a, b):
    return lax.dot_general(
        a, b, (((1,), (1,)), ((), ())), precision=HI, preferred_element_type=f32
    )


def lane_bcast(x, index):
    dims = lax.GatherDimensionNumbers(
        offset_dims=(), collapsed_slice_dims=(1,), start_index_map=(1,),
        operand_batching_dims=(0,), start_indices_batching_dims=(0,),
    )
    return lax.gather(
        x, index[:, :, None], dims, (1, 1), mode=lax.GatherScatterMode.PROMISE_IN_BOUNDS
    )


def row_bcast(row):
    return jnp.broadcast_to(row, (8, N))


def invert(d_ref, p_ref, q_ref):
    lane = lax.broadcasted_iota(jnp.int32, (8, N), 1)
    sub = lax.broadcasted_iota(jnp.int32, (8, N), 0)
    half = N // 2
    for h in (0, 1):
        top = h * half
        first = d_ref[top : top + 8, :]
        for j in range(8):
            p_ref[8 * j : 8 * j + 8, :] = lane_bcast(first, jnp.full((8, N), top + j, jnp.int32))

        def block(k, carry):
            base = pl.multiple_of(top + k * 8, 8)
            base_next = pl.multiple_of(top + jnp.minimum(k + 1, 7) * 8, 8)
            here = [jnp.full((8, N), base + j, jnp.int32) for j in range(8)]
            after = [jnp.full((8, N), base_next + j, jnp.int32) for j in range(8)]
            s = {}
            for j in range(8):
                for i in range(j + 1):
                    s[i, j] = row_bcast(p_ref[8 * j + i : 8 * j + i + 1, :])
            r = [row_bcast(d_ref[pl.ds(base + j, 1), :]) for j in range(8)]
            d = [d_ref[top + g * 8 : top + (g + 1) * 8, :] for g in range(8)]
            dn = d_ref[pl.ds(base_next, 8), :]
            cn, pn, c = [], [], []
            for j in range(8):
                cn.append(lane_bcast(dn, here[j]))
            for j in range(8):
                pn.append(lane_bcast(dn, after[j]))
            for j in range(8):
                c.append([lane_bcast(d[g], here[j]) for g in range(8)])
            inside = (lane >= base) & (lane < base + 8)
            r = [jnp.where(inside, jnp.where(lane == base + j, 1.0, 0.0), r[j]) for j in range(8)]
            low, inv = {}, []
            for j in range(8):
                inv.append(1.0 / s[j, j])
                for i in range(j + 1, 8):
                    low[i, j] = s[j, i] * inv[j]
                for i in range(j + 1, 8):
                    for m in range(i, 8):
                        s[i, m] = s[i, m] - low[i, j] * s[j, m]
                q_ref[8 * j : 8 * j + 8, :] = cn[j]
                scaled = cn[j] * inv[j]
                for i in range(8):
                    pn[i] = pn[i] - scaled * row_bcast(q_ref[8 * j + i : 8 * j + i + 1, :])
                for i in range(j + 1, 8):
                    cn[i] = cn[i] - low[i, j] * cn[j]
                for i in range(j + 1, 8):
                    r[i] = r[i] - low[i, j] * r[j]
            for j in range(8):
                p_ref[8 * j : 8 * j + 8, :] = pn[j]
            x = [r[j] * inv[j] for j in range(8)]
            for j in range(7, -1, -1):
                for i in range(j):
                    x[i] = x[i] - low[j, i] * x[j]
            for g in range(8):
                kept = jnp.where(inside, 0.0, d[g])
                t = [c[j][g] * x[j] for j in range(8)]
                d_ref[top + g * 8 : top + (g + 1) * 8, :] = kept - (
                    ((t[0] + t[1]) + (t[2] + t[3])) + ((t[4] + t[5]) + (t[6] + t[7]))
                )
            new = x[0]
            for j in range(1, 8):
                new = jnp.where(sub == j, x[j], new)
            d_ref[pl.ds(base, 8), :] = new
            return carry

        lax.fori_loop(0, 8, block, 0)
        wide = lax.broadcasted_iota(jnp.int32, (half, N), 1)
        if h == 0:
            rest = d_ref[half:N, :]
            d_ref[half:N, :] = jnp.where(wide < half, 0.0, rest) - dot(rest[:, 0:half], d_ref[0:half, :])
        else:
            rest = d_ref[0:half, :]
            d_ref[0:half, :] = jnp.where(wide < half, rest, 0.0) - dot(
                jnp.where(wide < half, 0.0, rest), d_ref[...]
            )


def kernel(
    parent, amat, coup, resid, nmat, nlink, nrhs, rmat, rrhs,
    packed,
    av, cv, bt, dinv, pbuf, qbuf, e1, rem1, e2, rem2, h3, wts,
    ntile, gath, snd, recv_y, acc_o, recv_c, acc_m, recv_z,
    nsys, nlinks, naug, hmat, rparts, send_r, recv_r, part, recv_g, tot, recv_t,
    msg, recv_n, zt, nd8,
    s_l, s_n, r_n, s_y, r_y, s_c, r_c, s_z, r_z, s_r, r_r, s_g, r_g, s_t, r_t, s_m, r_m,
):
    me = lax.axis_index("leaf")
    grp = lax.axis_index("grp")
    y, z, core = me // 16, (me // 2) % 8, me % 2
    own_z = 4 - grp // 4
    owner = z == own_z
    mine = 2 * y + core

    def dev(leaf):
        return {"leaf": leaf, "grp": grp}

    def owner_leaf(m, oz):
        return (m // 2) * 16 + oz * 2 + m % 2

    local = [
        pltpu.make_async_copy(amat.at[0, pl.ds(0, N), pl.ds(0, N)], dinv, s_l.at[0]),
        pltpu.make_async_copy(amat.at[0], av, s_l.at[1]),
        pltpu.make_async_copy(coup.at[0], cv, s_l.at[2]),
    ]
    for copy in local:
        copy.start()

    barrier = pltpu.get_barrier_semaphore()

    def greet(t, carry):
        pl.semaphore_signal(barrier, inc=1, device_id=dev((me + t) % 64), device_id_type=MESH)
        return carry

    lax.fori_loop(1, 64, greet, 0)

    @pl.when(owner)
    def _():
        def greet_far(t, carry):
            g = (grp + t) % 8
            pl.semaphore_signal(
                barrier, inc=1,
                device_id={"leaf": owner_leaf(mine, 4 - g // 4), "grp": g}, device_id_type=MESH,
            )
            return carry

        lax.fori_loop(1, 8, greet_far, 0)

    local[0].wait()
    invert(dinv, pbuf, qbuf)

    sub = lax.broadcasted_iota(jnp.int32, (8, N), 0)
    lane = lax.broadcasted_iota(jnp.int32, (8, N), 1)
    sub4 = lax.broadcasted_iota(jnp.int32, (4, N), 0)
    lane4 = lax.broadcasted_iota(jnp.int32, (4, N), 1)
    wts[...] = jnp.where(sub == parent[0], 1.0, 0.0)
    nd8[...] = jnp.zeros((8, N), f32)
    nd8[0:2, 0:8] = nrhs[...]
    pair = nd8[...]
    for q in range(8):
        value = lane_bcast(pair, jnp.full((8, N), q, jnp.int32))
        ntile[q, 0:2, :] = nmat[q]
        ntile[q, 2:4, :] = nlink[q]
        ntile[q, 4:8, :] = jnp.where(
            sub4 == 0,
            jnp.where(lane4 == 2 * me, value[0:1, :], 0.0)
            + jnp.where(lane4 == 2 * me + 1, value[1:2, :], 0.0),
            0.0,
        )

    @pl.when(owner)
    def _():
        pl.semaphore_wait(barrier, 70)

    @pl.when(jnp.logical_not(owner))
    def _():
        pl.semaphore_wait(barrier, 63)

    def node_copy(q, target):
        return pltpu.make_async_remote_copy(
            src_ref=ntile.at[q], dst_ref=gath.at[me], send_sem=s_n.at[q], recv_sem=r_n,
            device_id=dev(target), device_id_type=MESH,
        )

    for q in range(8):
        target = owner_leaf(q, own_z)

        @pl.when(target != me)
        def _():
            node_copy(q, target).start()

        @pl.when(target == me)
        def _():
            gath[me] = ntile[q]

    local[1].wait()
    local[2].wait()
    for b in range(3):
        bt[0:N, b * N : (b + 1) * N] = cv[b * N : (b + 1) * N, :].T
        bt[N:AUG, b * N : (b + 1) * N] = jnp.where(
            sub == 0, row_bcast(resid[:, b * N : (b + 1) * N]), 0.0
        )
    d1 = dinv[...]
    e1[0:256, :] = dot(av[N:384, 0:N], d1)
    e1[256:392, :] = dot(bt[:, 0:N], d1)
    snd[0:AUG, :] = dot_nt(e1[256:392, :], bt[0:N, 0:N])
    rem1[0:256, :] = av[N:384, N:384] - dot(e1[0:256, :], av[0:N, N:384])
    rem1[256:392, :] = bt[:, N:384] - dot(e1[256:392, :], av[0:N, N:384])
    dinv[...] = rem1[0:N, 0:N]
    invert(dinv, pbuf, qbuf)
    e2[...] = dot(rem1[N:392, 0:N], dinv[...])
    snd[0:AUG, :] += dot_nt(e2[N:264, :], rem1[256:384, 0:N])
    rem2[...] = rem1[N:392, N:256] - dot(e2[...], rem1[0:N, N:256])
    dinv[...] = rem2[0:N, :]
    invert(dinv, pbuf, qbuf)
    h3[...] = dot(rem2[N:264, :], dinv[...])
    snd[0:AUG, :] += dot_nt(h3[...], rem2[N:256, :])
    snd[AUG : AUG + 8, :] = wts[...]

    def y_copy(step, slot, part, src, sem):
        rows = pl.ds(72 * part, 72)
        return pltpu.make_async_remote_copy(
            src_ref=src.at[rows], dst_ref=recv_y.at[slot, rows], send_sem=s_y.at[sem],
            recv_sem=r_y.at[2 * slot + part],
            device_id=dev(((y + step + 4) % 4) * 16 + z * 2 + core), device_id_type=MESH,
        )

    up_a, up_b = y_copy(1, 0, 0, snd, 0), y_copy(1, 0, 1, snd, 1)
    down_b, down_a = y_copy(-1, 2, 1, snd, 2), y_copy(-1, 2, 0, snd, 3)
    pass_a = y_copy(1, 1, 0, recv_y.at[0], 4)
    pass_b = y_copy(-1, 1, 1, recv_y.at[2], 5)
    for copy in (up_a, down_b, up_b, down_a):
        copy.start()
    other = 2 * y + 1 - core
    acc_m[...] = snd[0:AUG, :] * snd[pl.ds(AUG + mine, 1), :]
    acc_o[...] = snd[0:AUG, :] * snd[pl.ds(AUG + other, 1), :]
    up_a.wait_recv()
    pass_a.start()
    down_b.wait_recv()
    pass_b.start()
    for slot, copies in ((0, (up_b,)), (2, (down_a,)), (1, (pass_a, pass_b))):
        for copy in copies:
            copy.wait_recv()
        acc_m[...] += recv_y[slot, 0:AUG, :] * recv_y[slot, pl.ds(AUG + mine, 1), :]
        acc_o[...] += recv_y[slot, 0:AUG, :] * recv_y[slot, pl.ds(AUG + other, 1), :]
    core_copy = pltpu.make_async_remote_copy(
        src_ref=acc_o, dst_ref=recv_c, send_sem=s_c, recv_sem=r_c,
        device_id=dev(me + 1 - 2 * core), device_id_type=MESH,
    )
    core_copy.start()
    core_copy.wait_recv()
    acc_m[...] += recv_c[...]

    def z_copy(source):
        return pltpu.make_async_remote_copy(
            src_ref=acc_m, dst_ref=recv_z.at[source], send_sem=s_z, recv_sem=r_z.at[source],
            device_id=dev(owner_leaf(mine, own_z)), device_id_type=MESH,
        )

    @pl.when(jnp.logical_not(owner))
    def _():
        z_copy(z).start()

    def slice_copy(src, dst, send_sem, recv_sem, t, by_group):
        if by_group:
            target = (grp + t) % 8
            device = {"leaf": owner_leaf(mine, 4 - target // 4), "grp": target}
            slot = grp
            source = src
        else:
            target = (mine + t) % 8
            device = dev(owner_leaf(target, own_z))
            slot = mine
            source = src
        return pltpu.make_async_remote_copy(
            src_ref=source, dst_ref=dst.at[slot], send_sem=send_sem.at[t], recv_sem=recv_sem.at[slot],
            device_id=device, device_id_type=MESH,
        )

    def slot_wait(dst, send_sem, recv_sem, slot):
        pltpu.make_async_remote_copy(
            src_ref=dst.at[slot], dst_ref=dst.at[slot], send_sem=send_sem.at[0],
            recv_sem=recv_sem.at[slot], device_id=dev(me + 1 - 2 * core), device_id_type=MESH,
        ).wait_recv()

    def message(far, t):
        plane = far + (7 - 2 * far) * (grp // 4)
        target = (mine + t) % 8
        return pltpu.make_async_remote_copy(
            src_ref=msg, dst_ref=recv_n.at[mine], send_sem=s_m.at[far, t], recv_sem=r_m.at[mine],
            device_id=dev((target // 2) * 16 + plane * 2 + target % 2), device_id_type=MESH,
        )

    @pl.when(owner)
    def _():
        pltpu.make_async_remote_copy(
            src_ref=gath.at[pl.ds(0, 63)], dst_ref=gath.at[pl.ds(0, 63)], send_sem=s_n.at[0],
            recv_sem=r_n, device_id=dev(me + 1 - 2 * core), device_id_type=MESH,
        ).wait_recv()
        rhs = jnp.zeros((4, N), f32)
        for i in range(64):
            tile = gath[i]
            nsys[2 * i : 2 * i + 2, :] = tile[0:2, :]
            nlinks[2 * i : 2 * i + 2, :] = tile[2:4, :]
            rhs = rhs + tile[4:8, :]
        naug[0:N, :] = nlinks[...].T
        acc_m[N : N + 4, :] += -rhs
        acc_m[0:N, :] += nsys[...]
        for t in (1, 7, 2, 6, 3, 5, 4):
            source = (own_z + t) % 8
            z_copy(source).wait_recv()
            acc_m[...] += recv_z[source]
        dinv[...] = acc_m[0:N, :]
        naug[N:AUG, :] = acc_m[N:AUG, :]
        invert(dinv, pbuf, qbuf)
        hmat[...] = dot(naug[...], dinv[...])
        rparts[...] = dot(hmat[...], nlinks[...])
        for q in range(8):
            send_r[q, 0:16, :] = rparts[16 * q : 16 * q + 16, :]
            send_r[q, 16:24, :] = rparts[N:AUG, :]

        for t in range(1, 8):
            slice_copy(send_r.at[(mine + t) % 8], recv_r, s_r, r_r, t, False).start()
        recv_r[mine] = send_r[mine]
        for t in range(1, 8):
            slot_wait(recv_r, s_r, r_r, (mine + t) % 8)
        total = recv_r[0]
        for q in range(1, 8):
            total = total + recv_r[q]
        part[...] = total
        for t in range(1, 8):
            slice_copy(part, recv_g, s_g, r_g, t, True).start()
        recv_g[grp] = total
        for t in range(1, 8):
            slot_wait(recv_g, s_g, r_g, (grp + t) % 8)
        total = recv_g[0]
        for q in range(1, 8):
            total = total + recv_g[q]
        tot[...] = total
        for t in range(1, 8):
            slice_copy(tot, recv_t, s_t, r_t, t, False).start()
        recv_t[mine] = total
        for t in range(1, 8):
            slot_wait(recv_t, s_t, r_t, (mine + t) % 8)
        for q in range(8):
            dinv[16 * q : 16 * q + 16, :] = rmat[16 * q : 16 * q + 16, :] + recv_t[q, 0:16, :]
        invert(dinv, pbuf, qbuf)
        root_vec = row_bcast(rrhs[...]) - row_bcast(total[16:17, :])
        root = dot(root_vec, dinv[...])
        node = row_bcast(hmat[N : N + 1, :]) + dot(root, hmat[0:N, :])
        msg[0:1, :] = node[0:1, :]
        msg[1:2, :] = root[0:1, :]

        for far in (0, 1, 7, 2, 6, 3, 5, 4):
            def send(t, carry):
                message(far, t).start()
                return carry

            lax.fori_loop(1 if far == 4 else 0, 8, send, 0)
        recv_n[mine] = msg[...]

    zt[:, 256:384] = h3[...]
    zt[:, N:256] = e2[N:264, :] - dot(h3[...], e2[0:N, :])
    zt[:, 0:N] = e1[256:392, :] - dot(zt[:, N:384], e1[0:256, :])

    @pl.when(owner)
    def _():
        for far in range(8):
            def drain(t, carry):
                message(far, t).wait_send()
                return carry

            lax.fori_loop(1 if far == 4 else 0, 8, drain, 0)

    for q in range(8):
        @pl.when(jnp.logical_or(jnp.logical_not(owner), mine != q))
        def _():
            slot_wait(recv_n, s_m, r_m, q)

    parent_dir = jnp.zeros((8, N), f32)
    for q in range(8):
        direction = row_bcast(recv_n[q, 0:1, :])
        parent_dir = parent_dir + direction * row_bcast(wts[q : q + 1, :])
        nd8[q : q + 1, :] = recv_n[q, 0:1, :]
    live = jnp.sum(wts[...], axis=0, keepdims=True)
    moved = dot(parent_dir, zt[0:N, :])
    for b in range(3):
        cols = slice(b * N, (b + 1) * N)
        packed[b : b + 1, :] = (zt[N : N + 1, cols] - moved[0:1, cols]) * live
    packed[3:4, :] = recv_n[0, 1:2, :]
    for a in range(2):
        values = lane_bcast(nd8[...], jnp.full((8, N), 2 * me + a, jnp.int32))
        packed[4 + a : 5 + a, :] = jnp.sum(jnp.where(sub == lane, values, 0.0), axis=0, keepdims=True)
    packed[6:8, :] = jnp.zeros((2, N), f32)

    for q in range(8):
        target = owner_leaf(q, own_z)

        @pl.when(target != me)
        def _():
            node_copy(q, target).wait_send()

    for copy in (up_a, up_b, down_a, down_b, pass_a, pass_b):
        copy.wait_send()
    core_copy.wait_send()

    @pl.when(jnp.logical_not(owner))
    def _():
        z_copy(z).wait_send()

    @pl.when(owner)
    def _():
        for t in range(1, 8):
            slice_copy(send_r.at[(mine + t) % 8], recv_r, s_r, r_r, t, False).wait_send()
            slice_copy(part, recv_g, s_g, r_g, t, True).wait_send()
            slice_copy(tot, recv_t, s_t, r_t, t, False).wait_send()


def unpack(packed, leaf_out, node_out, root_out):
    for b in range(3):
        leaf_out[:, b * N : (b + 1) * N] = packed[b : b + 1, :]
    node_out[...] = packed[4:6, 0:8]
    root_out[...] = packed[3:4, :]


def body(
    slot_parent, leaf_matrix, coupling, leaf_residual_rows, node_matrix, node_link, node_rhs,
    root_matrix, root_rhs,
):
    vmem = pl.BlockSpec(memory_space=pltpu.VMEM)
    buf = lambda *shape: pltpu.VMEM(shape, f32)
    dma = pltpu.SemaphoreType.DMA
    packed = pl.pallas_call(
        kernel,
        out_shape=jax.ShapeDtypeStruct((8, N), f32),
        in_specs=[
            pl.BlockSpec(memory_space=pltpu.SMEM), pl.BlockSpec(memory_space=pl.ANY),
            pl.BlockSpec(memory_space=pl.ANY),
        ] + [vmem] * 6,
        out_specs=vmem,
        scratch_shapes=[
            buf(384, 384), buf(384, N),
            buf(AUG, 384), buf(N, N), buf(64, N), buf(64, N), buf(392, N), buf(392, 256), buf(264, N),
            buf(264, N), buf(AUG, N), buf(8, N),
            buf(8, 8, N), buf(64, 8, N), buf(144, N), buf(3, 144, N), buf(AUG, N), buf(AUG, N),
            buf(AUG, N), buf(8, AUG, N),
            buf(N, N), buf(N, N), buf(AUG, N), buf(AUG, N), buf(AUG, N), buf(8, 24, N),
            buf(8, 24, N), buf(24, N), buf(8, 24, N), buf(24, N), buf(8, 24, N),
            buf(2, N), buf(8, 2, N), buf(AUG, 384), buf(8, N),
            dma((3,)), dma((8,)), dma, dma((6,)), dma((6,)), dma, dma, dma, dma((8,)),
            dma((8,)), dma((8,)), dma((8,)), dma((8,)), dma((8,)), dma((8,)), dma((8, 8)), dma((8,)),
        ],
        compiler_params=pltpu.CompilerParams(collective_id=0, has_side_effects=True),
        name="newton_step",
    )(
        slot_parent, leaf_matrix, coupling, leaf_residual_rows, node_matrix, node_link, node_rhs.T,
        root_matrix, root_rhs[None, :],
    )
    leaf_dir, node_dir, root_dir = pl.pallas_call(
        unpack,
        out_shape=(
            jax.ShapeDtypeStruct((1, 384), f32),
            jax.ShapeDtypeStruct((2, 8), f32),
            jax.ShapeDtypeStruct((1, N), f32),
        ),
        in_specs=[vmem],
        out_specs=(vmem, vmem, vmem),
        name="unpack",
    )(packed)
    return leaf_dir, node_dir.T, root_dir[0]


def solution(mesh):
    return jax.shard_map(
        body,
        mesh=mesh,
        in_specs=(
            P(("leaf", "grp")),
            P(("leaf", "grp"), None, None),
            P(("leaf", "grp"), None, None),
            P(("leaf", "grp"), None),
            P("grp", "leaf", None),
            P("grp", "leaf", None),
            P("grp", "leaf"),
            P(),
            P(),
        ),
        out_specs=(P(("leaf", "grp"), None), P("grp", "leaf"), P()),
        check_vma=False,
    )
```

```python
import jax
import jax.numpy as jnp
from jax import lax
from jax.experimental import pallas as pl
from jax.experimental.pallas import tpu as pltpu
from jax.sharding import PartitionSpec as P

f32 = jnp.float32
MESH = pl.DeviceIdType.MESH
HI = lax.Precision.HIGHEST
N = 128
AUG = 136
PANEL = 64
GROUPS = PANEL // 8


def dot(a, b):
    return jnp.dot(a, b, precision=HI, preferred_element_type=f32)


def dot_nt(a, b):
    return lax.dot_general(
        a, b, (((1,), (1,)), ((), ())), precision=HI, preferred_element_type=f32
    )


def lane_bcast(x, index):
    dims = lax.GatherDimensionNumbers(
        offset_dims=(), collapsed_slice_dims=(1,), start_index_map=(1,),
        operand_batching_dims=(0,), start_indices_batching_dims=(0,),
    )
    return lax.gather(
        x, index[:, :, None], dims, (1, 1), mode=lax.GatherScatterMode.PROMISE_IN_BOUNDS
    )


def row_bcast(row):
    return jnp.broadcast_to(row, (8, N))


def invert(d_ref, p_ref, q_ref):
    lane = lax.broadcasted_iota(jnp.int32, (8, N), 1)
    sub = lax.broadcasted_iota(jnp.int32, (8, N), 0)
    for h in range(N // PANEL):
        top = h * PANEL
        first = d_ref[top : top + 8, :]
        for j in range(8):
            p_ref[8 * j : 8 * j + 8, :] = lane_bcast(first, jnp.full((8, N), top + j, jnp.int32))

        for k in range(GROUPS):
            base = top + k * 8
            base_next = top + min(k + 1, GROUPS - 1) * 8
            here = [jnp.full((8, N), base + j, jnp.int32) for j in range(8)]
            after = [jnp.full((8, N), base_next + j, jnp.int32) for j in range(8)]
            s = {}
            for j in range(8):
                for i in range(j + 1):
                    s[i, j] = row_bcast(p_ref[8 * j + i : 8 * j + i + 1, :])
            r = [row_bcast(d_ref[pl.ds(base + j, 1), :]) for j in range(8)]
            d = [d_ref[top + g * 8 : top + (g + 1) * 8, :] for g in range(GROUPS)]
            dn = d_ref[pl.ds(base_next, 8), :]
            cn, pn, c = [], [], []
            for j in range(8):
                cn.append(lane_bcast(dn, here[j]))
            for j in range(8):
                pn.append(lane_bcast(dn, after[j]))
            for j in range(8):
                c.append([lane_bcast(d[g], here[j]) for g in range(GROUPS)])
            inside = (lane >= base) & (lane < base + 8)
            r = [jnp.where(inside, jnp.where(lane == base + j, 1.0, 0.0), r[j]) for j in range(8)]
            low, inv = {}, []
            for j in range(8):
                inv.append(1.0 / s[j, j])
                for i in range(j + 1, 8):
                    low[i, j] = s[j, i] * inv[j]
                for i in range(j + 1, 8):
                    for m in range(i, 8):
                        s[i, m] = s[i, m] - low[i, j] * s[j, m]
                q_ref[8 * j : 8 * j + 8, :] = cn[j]
                scaled = cn[j] * inv[j]
                for i in range(8):
                    pn[i] = pn[i] - scaled * row_bcast(q_ref[8 * j + i : 8 * j + i + 1, :])
                for i in range(j + 1, 8):
                    cn[i] = cn[i] - low[i, j] * cn[j]
                for i in range(j + 1, 8):
                    r[i] = r[i] - low[i, j] * r[j]
            for j in range(8):
                p_ref[8 * j : 8 * j + 8, :] = pn[j]
            x = [r[j] * inv[j] for j in range(8)]
            for j in range(7, -1, -1):
                for i in range(j):
                    x[i] = x[i] - low[j, i] * x[j]
            for g in range(GROUPS):
                kept = jnp.where(inside, 0.0, d[g])
                t = [c[j][g] * x[j] for j in range(8)]
                d_ref[top + g * 8 : top + (g + 1) * 8, :] = kept - (
                    ((t[0] + t[1]) + (t[2] + t[3])) + ((t[4] + t[5]) + (t[6] + t[7]))
                )
            new = x[0]
            for j in range(1, 8):
                new = jnp.where(sub == j, x[j], new)
            d_ref[pl.ds(base, 8), :] = new
        pan = d_ref[top : top + PANEL, :]
        wide = lax.broadcasted_iota(jnp.int32, (N - PANEL, N), 1)
        in_pan = (wide >= top) & (wide < top + PANEL)
        if top == 0:
            rest = d_ref[PANEL:N, :]
        elif top + PANEL == N:
            rest = d_ref[0:top, :]
        else:
            rest = jnp.concatenate([d_ref[0:top, :], d_ref[top + PANEL : N, :]], axis=0)
        out = jnp.where(in_pan, 0.0, rest) - dot(rest[:, top : top + PANEL], pan)
        if top > 0:
            d_ref[0:top, :] = out[0:top, :]
        if top + PANEL < N:
            d_ref[top + PANEL : N, :] = out[top : N - PANEL, :]


def kernel(
    parent, amat, coup, resid, nmat, nlink, nrhs, rmat, rrhs,
    packed,
    av, cv, bt, dinv, dinv2, dinv3, pbuf, qbuf, pbuf2, qbuf2, e1, rem1, e2, rem2, h3, wts,
    ntile, gath, snd, recv_y, acc_o, recv_c, acc_m, recv_z,
    nsys, nvec, nlinks, naug, hmat, rparts, send_r, recv_r, part, recv_g, tot, recv_t,
    msg, recv_n, zt, nd8,
    s_l, s_n, r_n, s_y, r_y, s_c, r_c, s_z, r_z, s_r, r_r, s_g, r_g, s_t, r_t, s_m, r_m,
):
    me = lax.axis_index("leaf")
    grp = lax.axis_index("grp")
    y, z, core = me // 16, (me // 2) % 8, me % 2
    own_z = 4 - grp // 4
    owner = z == own_z
    mine = 2 * y + core

    def dev(leaf):
        return {"leaf": leaf, "grp": grp}

    def owner_leaf(m, oz):
        return (m // 2) * 16 + oz * 2 + m % 2

    local = [
        pltpu.make_async_copy(amat.at[0, pl.ds(0, N), pl.ds(0, N)], dinv, s_l.at[0]),
        pltpu.make_async_copy(amat.at[0], av, s_l.at[1]),
        pltpu.make_async_copy(coup.at[0], cv, s_l.at[2]),
    ]
    for copy in local:
        copy.start()

    barrier = pltpu.get_barrier_semaphore()

    def greet(t, carry):
        pl.semaphore_signal(barrier, inc=1, device_id=dev((me + t) % 64), device_id_type=MESH)
        return carry

    lax.fori_loop(1, 64, greet, 0)

    @pl.when(owner)
    def _():
        def greet_far(t, carry):
            g = (grp + t) % 8
            pl.semaphore_signal(
                barrier, inc=1,
                device_id={"leaf": owner_leaf(mine, 4 - g // 4), "grp": g}, device_id_type=MESH,
            )
            return carry

        lax.fori_loop(1, 8, greet_far, 0)

    local[0].wait()
    invert(dinv, pbuf, qbuf)

    sub = lax.broadcasted_iota(jnp.int32, (8, N), 0)
    lane = lax.broadcasted_iota(jnp.int32, (8, N), 1)
    sub4 = lax.broadcasted_iota(jnp.int32, (4, N), 0)
    lane4 = lax.broadcasted_iota(jnp.int32, (4, N), 1)
    wts[...] = jnp.where(sub == parent[0], 1.0, 0.0)
    nd8[...] = jnp.zeros((8, N), f32)
    nd8[0:2, 0:8] = nrhs[...]
    pair = nd8[...]
    for q in range(8):
        value = lane_bcast(pair, jnp.full((8, N), q, jnp.int32))
        ntile[q, 0:2, :] = nmat[q]
        ntile[q, 2:4, :] = nlink[q]
        ntile[q, 4:8, :] = jnp.where(
            sub4 == 0,
            jnp.where(lane4 == 2 * me, value[0:1, :], 0.0)
            + jnp.where(lane4 == 2 * me + 1, value[1:2, :], 0.0),
            0.0,
        )

    @pl.when(owner)
    def _():
        pl.semaphore_wait(barrier, 70)

    @pl.when(jnp.logical_not(owner))
    def _():
        pl.semaphore_wait(barrier, 63)

    def node_copy(q, target):
        return pltpu.make_async_remote_copy(
            src_ref=ntile.at[q], dst_ref=gath.at[me], send_sem=s_n.at[q], recv_sem=r_n,
            device_id=dev(target), device_id_type=MESH,
        )

    for q in range(8):
        target = owner_leaf(q, own_z)

        @pl.when(target != me)
        def _():
            node_copy(q, target).start()

        @pl.when(target == me)
        def _():
            gath[me] = ntile[q]

    local[1].wait()
    local[2].wait()
    for b in range(3):
        bt[0:N, b * N : (b + 1) * N] = cv[b * N : (b + 1) * N, :].T
        bt[N:AUG, b * N : (b + 1) * N] = jnp.where(
            sub == 0, row_bcast(resid[:, b * N : (b + 1) * N]), 0.0
        )
    e1[0:N, :] = dot(av[N:256, 0:N], dinv[...])
    dinv2[...] = av[N:256, N:256] - dot(e1[0:N, :], av[0:N, N:256])
    e1[N:392, :] = dot(jnp.concatenate([av[256:384, 0:N], bt[:, 0:N]], axis=0), dinv[...])
    rem1[0:N, N:256] = av[N:256, 256:384] - dot(e1[0:N, :], av[0:N, 256:384])
    rem1[N:256, :] = av[256:384, N:384] - dot(e1[N:256, :], av[0:N, N:384])
    rem1[256:392, :] = bt[:, N:384] - dot(e1[256:392, :], av[0:N, N:384])
    snd[0:AUG, :] = dot_nt(e1[256:392, :], bt[0:N, 0:N])
    invert(dinv2, pbuf2, qbuf2)
    e2[0:N, :] = dot(rem1[N:256, 0:N], dinv2[...])
    dinv3[...] = rem1[N:256, N:256] - dot(e2[0:N, :], rem1[0:N, N:256])
    e2[N:264, :] = dot(rem1[256:392, 0:N], dinv2[...])
    rem2[...] = rem1[256:392, N:256] - dot(e2[N:264, :], rem1[0:N, N:256])
    snd[0:AUG, :] += dot_nt(e2[N:264, :], rem1[256:384, 0:N])
    invert(dinv3, pbuf, qbuf)
    h3[...] = dot(rem2[...], dinv3[...])
    snd[0:AUG, :] += dot_nt(h3[...], rem2[0:N, :])
    snd[AUG : AUG + 8, :] = wts[...]

    def y_copy(step, slot, part, src, sem):
        rows = pl.ds(72 * part, 72)
        return pltpu.make_async_remote_copy(
            src_ref=src.at[rows], dst_ref=recv_y.at[slot, rows], send_sem=s_y.at[sem],
            recv_sem=r_y.at[2 * slot + part],
            device_id=dev(((y + step + 4) % 4) * 16 + z * 2 + core), device_id_type=MESH,
        )

    up_a, up_b = y_copy(1, 0, 0, snd, 0), y_copy(1, 0, 1, snd, 1)
    down_b, down_a = y_copy(-1, 2, 1, snd, 2), y_copy(-1, 2, 0, snd, 3)
    pass_a = y_copy(1, 1, 0, recv_y.at[0], 4)
    pass_b = y_copy(-1, 1, 1, recv_y.at[2], 5)
    for copy in (up_a, down_b, up_b, down_a):
        copy.start()

    zt[:, 256:384] = h3[...]
    zt[:, N:256] = e2[N:264, :] - dot(h3[...], e2[0:N, :])
    zt[:, 0:N] = e1[256:392, :] - dot(zt[:, N:384], e1[0:256, :])

    @pl.when(owner)
    def _():
        pltpu.make_async_remote_copy(
            src_ref=gath.at[pl.ds(0, 63)], dst_ref=gath.at[pl.ds(0, 63)], send_sem=s_n.at[0],
            recv_sem=r_n, device_id=dev(me + 1 - 2 * core), device_id_type=MESH,
        ).wait_recv()
        rhs = jnp.zeros((4, N), f32)
        for i in range(64):
            tile = gath[i]
            nsys[2 * i : 2 * i + 2, :] = tile[0:2, :]
            nlinks[2 * i : 2 * i + 2, :] = tile[2:4, :]
            rhs = rhs + tile[4:8, :]
        naug[0:N, :] = nlinks[...].T
        nvec[...] = rhs

    other = 2 * y + 1 - core
    acc_m[...] = snd[0:AUG, :] * snd[pl.ds(AUG + mine, 1), :]
    acc_o[...] = snd[0:AUG, :] * snd[pl.ds(AUG + other, 1), :]
    up_a.wait_recv()
    pass_a.start()
    down_b.wait_recv()
    pass_b.start()
    for slot, copies in ((0, (up_b,)), (2, (down_a,)), (1, (pass_a, pass_b))):
        for copy in copies:
            copy.wait_recv()
        acc_m[...] += recv_y[slot, 0:AUG, :] * recv_y[slot, pl.ds(AUG + mine, 1), :]
        acc_o[...] += recv_y[slot, 0:AUG, :] * recv_y[slot, pl.ds(AUG + other, 1), :]
    core_copy = pltpu.make_async_remote_copy(
        src_ref=acc_o, dst_ref=recv_c, send_sem=s_c, recv_sem=r_c,
        device_id=dev(me + 1 - 2 * core), device_id_type=MESH,
    )
    core_copy.start()
    core_copy.wait_recv()
    acc_m[...] += recv_c[...]

    def z_copy(source):
        return pltpu.make_async_remote_copy(
            src_ref=acc_m, dst_ref=recv_z.at[source], send_sem=s_z, recv_sem=r_z.at[source],
            device_id=dev(owner_leaf(mine, own_z)), device_id_type=MESH,
        )

    @pl.when(jnp.logical_not(owner))
    def _():
        z_copy(z).start()

    def slice_copy(src, dst, send_sem, recv_sem, t, by_group):
        if by_group:
            target = (grp + t) % 8
            device = {"leaf": owner_leaf(mine, 4 - target // 4), "grp": target}
            slot = grp
            source = src
        else:
            target = (mine + t) % 8
            device = dev(owner_leaf(target, own_z))
            slot = mine
            source = src
        return pltpu.make_async_remote_copy(
            src_ref=source, dst_ref=dst.at[slot], send_sem=send_sem.at[t], recv_sem=recv_sem.at[slot],
            device_id=device, device_id_type=MESH,
        )

    def slot_wait(dst, send_sem, recv_sem, slot):
        pltpu.make_async_remote_copy(
            src_ref=dst.at[slot], dst_ref=dst.at[slot], send_sem=send_sem.at[0],
            recv_sem=recv_sem.at[slot], device_id=dev(me + 1 - 2 * core), device_id_type=MESH,
        ).wait_recv()

    def message(far, t):
        plane = far + (7 - 2 * far) * (grp // 4)
        target = (mine + t) % 8
        return pltpu.make_async_remote_copy(
            src_ref=msg, dst_ref=recv_n.at[mine], send_sem=s_m.at[far, t], recv_sem=r_m.at[mine],
            device_id=dev((target // 2) * 16 + plane * 2 + target % 2), device_id_type=MESH,
        )

    @pl.when(owner)
    def _():
        acc_m[N : N + 4, :] += -nvec[...]
        acc_m[0:N, :] += nsys[...]
        for t in (1, 7, 2, 6, 3, 5, 4):
            source = (own_z + t) % 8
            z_copy(source).wait_recv()
            acc_m[...] += recv_z[source]
        dinv[...] = acc_m[0:N, :]
        naug[N:AUG, :] = acc_m[N:AUG, :]
        invert(dinv, pbuf, qbuf)
        hmat[...] = dot(naug[...], dinv[...])
        rparts[...] = dot(hmat[...], nlinks[...])
        for q in range(8):
            send_r[q, 0:16, :] = rparts[16 * q : 16 * q + 16, :]
            send_r[q, 16:24, :] = rparts[N:AUG, :]

        for t in range(1, 8):
            slice_copy(send_r.at[(mine + t) % 8], recv_r, s_r, r_r, t, False).start()
        recv_r[mine] = send_r[mine]
        for t in range(1, 8):
            slot_wait(recv_r, s_r, r_r, (mine + t) % 8)
        total = recv_r[0]
        for q in range(1, 8):
            total = total + recv_r[q]
        part[...] = total
        for t in range(1, 8):
            slice_copy(part, recv_g, s_g, r_g, t, True).start()
        recv_g[grp] = total
        for t in range(1, 8):
            slot_wait(recv_g, s_g, r_g, (grp + t) % 8)
        total = recv_g[0]
        for q in range(1, 8):
            total = total + recv_g[q]
        tot[...] = total
        for t in range(1, 8):
            slice_copy(tot, recv_t, s_t, r_t, t, False).start()
        recv_t[mine] = total
        for t in range(1, 8):
            slot_wait(recv_t, s_t, r_t, (mine + t) % 8)
        for q in range(8):
            dinv[16 * q : 16 * q + 16, :] = rmat[16 * q : 16 * q + 16, :] + recv_t[q, 0:16, :]
        invert(dinv, pbuf, qbuf)
        root_vec = row_bcast(rrhs[...]) - row_bcast(total[16:17, :])
        root = dot(root_vec, dinv[...])
        node = row_bcast(hmat[N : N + 1, :]) + dot(root, hmat[0:N, :])
        msg[0:1, :] = node[0:1, :]
        msg[1:2, :] = root[0:1, :]

        for far in (0, 1, 7, 2, 6, 3, 5, 4):
            def send(t, carry):
                message(far, t).start()
                return carry

            lax.fori_loop(1 if far == 4 else 0, 8, send, 0)
        recv_n[mine] = msg[...]

    @pl.when(owner)
    def _():
        for far in range(8):
            def drain(t, carry):
                message(far, t).wait_send()
                return carry

            lax.fori_loop(1 if far == 4 else 0, 8, drain, 0)

    for q in range(8):
        @pl.when(jnp.logical_or(jnp.logical_not(owner), mine != q))
        def _():
            slot_wait(recv_n, s_m, r_m, q)

    parent_dir = jnp.zeros((8, N), f32)
    for q in range(8):
        direction = row_bcast(recv_n[q, 0:1, :])
        parent_dir = parent_dir + direction * row_bcast(wts[q : q + 1, :])
        nd8[q : q + 1, :] = recv_n[q, 0:1, :]
    live = jnp.sum(wts[...], axis=0, keepdims=True)
    moved = dot(parent_dir, zt[0:N, :])
    for b in range(3):
        cols = slice(b * N, (b + 1) * N)
        packed[b : b + 1, :] = (zt[N : N + 1, cols] - moved[0:1, cols]) * live
    packed[3:4, :] = recv_n[0, 1:2, :]
    for a in range(2):
        values = lane_bcast(nd8[...], jnp.full((8, N), 2 * me + a, jnp.int32))
        packed[4 + a : 5 + a, :] = jnp.sum(jnp.where(sub == lane, values, 0.0), axis=0, keepdims=True)
    packed[6:8, :] = jnp.zeros((2, N), f32)

    for q in range(8):
        target = owner_leaf(q, own_z)

        @pl.when(target != me)
        def _():
            node_copy(q, target).wait_send()

    for copy in (up_a, up_b, down_a, down_b, pass_a, pass_b):
        copy.wait_send()
    core_copy.wait_send()

    @pl.when(jnp.logical_not(owner))
    def _():
        z_copy(z).wait_send()

    @pl.when(owner)
    def _():
        for t in range(1, 8):
            slice_copy(send_r.at[(mine + t) % 8], recv_r, s_r, r_r, t, False).wait_send()
            slice_copy(part, recv_g, s_g, r_g, t, True).wait_send()
            slice_copy(tot, recv_t, s_t, r_t, t, False).wait_send()


def unpack(packed, leaf_out, node_out, root_out):
    for b in range(3):
        leaf_out[:, b * N : (b + 1) * N] = packed[b : b + 1, :]
    node_out[...] = packed[4:6, 0:8]
    root_out[...] = packed[3:4, :]


def body(
    slot_parent, leaf_matrix, coupling, leaf_residual_rows, node_matrix, node_link, node_rhs,
    root_matrix, root_rhs,
):
    vmem = pl.BlockSpec(memory_space=pltpu.VMEM)
    buf = lambda *shape: pltpu.VMEM(shape, f32)
    dma = pltpu.SemaphoreType.DMA
    packed = pl.pallas_call(
        kernel,
        out_shape=jax.ShapeDtypeStruct((8, N), f32),
        in_specs=[
            pl.BlockSpec(memory_space=pltpu.SMEM), pl.BlockSpec(memory_space=pl.ANY),
            pl.BlockSpec(memory_space=pl.ANY),
        ] + [vmem] * 6,
        out_specs=vmem,
        scratch_shapes=[
            buf(384, 384), buf(384, N),
            buf(AUG, 384), buf(N, N), buf(N, N), buf(N, N), buf(64, N), buf(64, N), buf(64, N), buf(64, N),
            buf(392, N), buf(392, 256), buf(264, N), buf(AUG, N), buf(AUG, N), buf(8, N),
            buf(8, 8, N), buf(64, 8, N), buf(144, N), buf(3, 144, N), buf(AUG, N), buf(AUG, N),
            buf(AUG, N), buf(8, AUG, N),
            buf(N, N), buf(4, N), buf(N, N), buf(AUG, N), buf(AUG, N), buf(AUG, N), buf(8, 24, N),
            buf(8, 24, N), buf(24, N), buf(8, 24, N), buf(24, N), buf(8, 24, N),
            buf(2, N), buf(8, 2, N), buf(AUG, 384), buf(8, N),
            dma((3,)), dma((8,)), dma, dma((6,)), dma((6,)), dma, dma, dma, dma((8,)),
            dma((8,)), dma((8,)), dma((8,)), dma((8,)), dma((8,)), dma((8,)), dma((8, 8)), dma((8,)),
        ],
        compiler_params=pltpu.CompilerParams(collective_id=0, has_side_effects=True),
        name="newton_step",
    )(
        slot_parent, leaf_matrix, coupling, leaf_residual_rows, node_matrix, node_link, node_rhs.T,
        root_matrix, root_rhs[None, :],
    )
    leaf_dir, node_dir, root_dir = pl.pallas_call(
        unpack,
        out_shape=(
            jax.ShapeDtypeStruct((1, 384), f32),
            jax.ShapeDtypeStruct((2, 8), f32),
            jax.ShapeDtypeStruct((1, N), f32),
        ),
        in_specs=[vmem],
        out_specs=(vmem, vmem, vmem),
        name="unpack",
    )(packed)
    return leaf_dir, node_dir.T, root_dir[0]


def solution(mesh):
    return jax.shard_map(
        body,
        mesh=mesh,
        in_specs=(
            P(("leaf", "grp")),
            P(("leaf", "grp"), None, None),
            P(("leaf", "grp"), None, None),
            P(("leaf", "grp"), None),
            P("grp", "leaf", None),
            P("grp", "leaf", None),
            P("grp", "leaf"),
            P(),
            P(),
        ),
        out_specs=(P(("leaf", "grp"), None), P("grp", "leaf"), P()),
        check_vma=False,
    )
```

```python
import jax
import jax.numpy as jnp
from jax import lax
from jax.experimental import pallas as pl
from jax.experimental.pallas import tpu as pltpu
from jax.sharding import PartitionSpec as P

f32 = jnp.float32
MESH = pl.DeviceIdType.MESH
HI = lax.Precision.HIGHEST
N = 128
AUG = 136
PANEL = 64
GROUPS = PANEL // 8


def rem(a, b):
    return a % b if isinstance(a, int) else lax.rem(a, b)


def div(a, b):
    return a // b if isinstance(a, int) else lax.div(a, b)


def dot(a, b):
    return jnp.dot(a, b, precision=HI, preferred_element_type=f32)


def dot_nt(a, b):
    return lax.dot_general(
        a, b, (((1,), (1,)), ((), ())), precision=HI, preferred_element_type=f32
    )


def lane_bcast(x, index):
    dims = lax.GatherDimensionNumbers(
        offset_dims=(), collapsed_slice_dims=(1,), start_index_map=(1,),
        operand_batching_dims=(0,), start_indices_batching_dims=(0,),
    )
    return lax.gather(
        x, index[:, :, None], dims, (1, 1), mode=lax.GatherScatterMode.PROMISE_IN_BOUNDS
    )


def row_bcast(row):
    return jnp.broadcast_to(row, (8, N))


def invert(d_ref, p_ref, q_ref):
    lane = lax.broadcasted_iota(jnp.int32, (8, N), 1)
    sub = lax.broadcasted_iota(jnp.int32, (8, N), 0)
    for h in range(N // PANEL):
        top = h * PANEL
        first = d_ref[top : top + 8, :]
        for j in range(8):
            p_ref[8 * j : 8 * j + 8, :] = lane_bcast(first, jnp.full((8, N), top + j, jnp.int32))

        for k in range(GROUPS):
            base = top + k * 8
            base_next = top + min(k + 1, GROUPS - 1) * 8
            here = [jnp.full((8, N), base + j, jnp.int32) for j in range(8)]
            after = [jnp.full((8, N), base_next + j, jnp.int32) for j in range(8)]
            s = {}
            for j in range(8):
                for i in range(j + 1):
                    s[i, j] = row_bcast(p_ref[8 * j + i : 8 * j + i + 1, :])
            r = [row_bcast(d_ref[pl.ds(base + j, 1), :]) for j in range(8)]
            d = [d_ref[top + g * 8 : top + (g + 1) * 8, :] for g in range(GROUPS)]
            dn = d_ref[pl.ds(base_next, 8), :]
            cn, pn, c = [], [], []
            for j in range(8):
                cn.append(lane_bcast(dn, here[j]))
            for j in range(8):
                pn.append(lane_bcast(dn, after[j]))
            for j in range(8):
                c.append([lane_bcast(d[g], here[j]) for g in range(GROUPS)])
            inside = (lane >= base) & (lane < base + 8)
            r = [jnp.where(inside, jnp.where(lane == base + j, 1.0, 0.0), r[j]) for j in range(8)]
            low, inv = {}, []
            for j in range(8):
                inv.append(1.0 / s[j, j])
                for i in range(j + 1, 8):
                    low[i, j] = s[j, i] * inv[j]
                for i in range(j + 1, 8):
                    for m in range(i, 8):
                        s[i, m] = s[i, m] - low[i, j] * s[j, m]
                q_ref[8 * j : 8 * j + 8, :] = cn[j]
                scaled = cn[j] * inv[j]
                for i in range(8):
                    pn[i] = pn[i] - scaled * row_bcast(q_ref[8 * j + i : 8 * j + i + 1, :])
                for i in range(j + 1, 8):
                    cn[i] = cn[i] - low[i, j] * cn[j]
                for i in range(j + 1, 8):
                    r[i] = r[i] - low[i, j] * r[j]
            for j in range(8):
                p_ref[8 * j : 8 * j + 8, :] = pn[j]
            x = [r[j] * inv[j] for j in range(8)]
            for j in range(7, -1, -1):
                for i in range(j):
                    x[i] = x[i] - low[j, i] * x[j]
            for g in range(GROUPS):
                kept = jnp.where(inside, 0.0, d[g])
                t = [c[j][g] * x[j] for j in range(8)]
                d_ref[top + g * 8 : top + (g + 1) * 8, :] = kept - (
                    ((t[0] + t[1]) + (t[2] + t[3])) + ((t[4] + t[5]) + (t[6] + t[7]))
                )
            new = x[0]
            for j in range(1, 8):
                new = jnp.where(sub == j, x[j], new)
            d_ref[pl.ds(base, 8), :] = new
        pan = d_ref[top : top + PANEL, :]
        wide = lax.broadcasted_iota(jnp.int32, (N - PANEL, N), 1)
        in_pan = (wide >= top) & (wide < top + PANEL)
        if top == 0:
            rest = d_ref[PANEL:N, :]
        elif top + PANEL == N:
            rest = d_ref[0:top, :]
        else:
            rest = jnp.concatenate([d_ref[0:top, :], d_ref[top + PANEL : N, :]], axis=0)
        out = jnp.where(in_pan, 0.0, rest) - dot(rest[:, top : top + PANEL], pan)
        if top > 0:
            d_ref[0:top, :] = out[0:top, :]
        if top + PANEL < N:
            d_ref[top + PANEL : N, :] = out[top : N - PANEL, :]


def kernel(
    parent, amat, coup, resid, nmat, nlink, nrhs, rmat, rrhs,
    packed,
    av, cv, bt, dinv, dinv2, dinv3, pbuf, qbuf, pbuf2, qbuf2, e1, rem1, e2, rem2, h3, wts,
    ntile, gath, snd, recv_y, acc_o, recv_c, acc_m, recv_z,
    nsys, nvec, nlinks, naug, hmat, rparts, send_r, recv_r, part, recv_g, tot, recv_t,
    msg, recv_n, zt, nd8,
    s_l, s_n, r_n, s_y, r_y, s_c, r_c, s_z, r_z, s_r, r_r, s_g, r_g, s_t, r_t, s_m, r_m,
):
    me = lax.axis_index("leaf")
    grp = lax.axis_index("grp")
    y, z, core = div(me, 16), rem(div(me, 2), 8), rem(me, 2)
    z_half = div(grp, 4)
    own_z = 4 - z_half
    owner = z == own_z
    mine = 2 * y + core

    def dev(leaf):
        return {"leaf": leaf, "grp": grp}

    def owner_leaf(m, oz):
        return div(m, 2) * 16 + oz * 2 + rem(m, 2)

    local = [
        pltpu.make_async_copy(amat.at[0, pl.ds(0, N), pl.ds(0, N)], dinv, s_l.at[0]),
        pltpu.make_async_copy(amat.at[0], av, s_l.at[1]),
        pltpu.make_async_copy(coup.at[0], cv, s_l.at[2]),
    ]
    for copy in local:
        copy.start()

    barrier = pltpu.get_barrier_semaphore()

    def greet(leaf):
        pl.semaphore_signal(barrier, inc=1, device_id=dev(leaf), device_id_type=MESH)

    @pl.when(jnp.logical_not(owner))
    def _():
        for step in (1, 3):
            greet(rem(y + step, 4) * 16 + z * 2 + core)
        greet(me + 1 - 2 * core)
        for q in range(8):
            greet(owner_leaf(q, own_z))

    @pl.when(owner)
    def _():
        def greet_all(t, carry):
            greet(rem(me + t, 64))
            return carry

        lax.fori_loop(1, 64, greet_all, 0)

        def greet_far(t, carry):
            g = rem(grp + t, 8)
            pl.semaphore_signal(
                barrier, inc=1,
                device_id={"leaf": owner_leaf(mine, 4 - div(g, 4)), "grp": g}, device_id_type=MESH,
            )
            return carry

        lax.fori_loop(1, 8, greet_far, 0)

    local[0].wait()
    invert(dinv, pbuf, qbuf)

    sub = lax.broadcasted_iota(jnp.int32, (8, N), 0)
    lane = lax.broadcasted_iota(jnp.int32, (8, N), 1)
    sub4 = lax.broadcasted_iota(jnp.int32, (4, N), 0)
    lane4 = lax.broadcasted_iota(jnp.int32, (4, N), 1)
    wts[...] = jnp.where(sub == parent[0], 1.0, 0.0)
    nd8[...] = jnp.zeros((8, N), f32)
    nd8[0:2, 0:8] = nrhs[...]
    pair = nd8[...]
    for q in range(8):
        value = lane_bcast(pair, jnp.full((8, N), q, jnp.int32))
        ntile[q, 0:2, :] = nmat[q]
        ntile[q, 2:4, :] = nlink[q]
        ntile[q, 4:8, :] = jnp.where(
            sub4 == 0,
            jnp.where(lane4 == 2 * me, value[0:1, :], 0.0)
            + jnp.where(lane4 == 2 * me + 1, value[1:2, :], 0.0),
            0.0,
        )

    @pl.when(owner)
    def _():
        pl.semaphore_wait(barrier, 70)

    @pl.when(jnp.logical_not(owner))
    def _():
        pl.semaphore_wait(barrier, 11)

    def node_copy(q, target):
        return pltpu.make_async_remote_copy(
            src_ref=ntile.at[q], dst_ref=gath.at[me], send_sem=s_n.at[q], recv_sem=r_n,
            device_id=dev(target), device_id_type=MESH,
        )

    for q in range(8):
        target = owner_leaf(q, own_z)

        @pl.when(target != me)
        def _():
            node_copy(q, target).start()

        @pl.when(target == me)
        def _():
            gath[me] = ntile[q]

    local[1].wait()
    local[2].wait()
    for b in range(3):
        bt[0:N, b * N : (b + 1) * N] = cv[b * N : (b + 1) * N, :].T
        bt[N:AUG, b * N : (b + 1) * N] = jnp.where(
            sub == 0, row_bcast(resid[:, b * N : (b + 1) * N]), 0.0
        )
    e1[0:N, :] = dot(av[N:256, 0:N], dinv[...])
    dinv2[...] = av[N:256, N:256] - dot(e1[0:N, :], av[0:N, N:256])
    e1[N:392, :] = dot(jnp.concatenate([av[256:384, 0:N], bt[:, 0:N]], axis=0), dinv[...])
    rem1[0:N, N:256] = av[N:256, 256:384] - dot(e1[0:N, :], av[0:N, 256:384])
    rem1[N:256, :] = av[256:384, N:384] - dot(e1[N:256, :], av[0:N, N:384])
    rem1[256:392, :] = bt[:, N:384] - dot(e1[256:392, :], av[0:N, N:384])
    snd[0:AUG, :] = dot_nt(e1[256:392, :], bt[0:N, 0:N])
    invert(dinv2, pbuf2, qbuf2)
    e2[0:N, :] = dot(rem1[N:256, 0:N], dinv2[...])
    dinv3[...] = rem1[N:256, N:256] - dot(e2[0:N, :], rem1[0:N, N:256])
    e2[N:264, :] = dot(rem1[256:392, 0:N], dinv2[...])
    rem2[...] = rem1[256:392, N:256] - dot(e2[N:264, :], rem1[0:N, N:256])
    snd[0:AUG, :] += dot_nt(e2[N:264, :], rem1[256:384, 0:N])
    invert(dinv3, pbuf, qbuf)
    h3[...] = dot(rem2[...], dinv3[...])
    snd[0:AUG, :] += dot_nt(h3[...], rem2[0:N, :])
    snd[AUG : AUG + 8, :] = wts[...]

    def y_copy(step, slot, part, src, sem):
        rows = pl.ds(72 * part, 72)
        return pltpu.make_async_remote_copy(
            src_ref=src.at[rows], dst_ref=recv_y.at[slot, rows], send_sem=s_y.at[sem],
            recv_sem=r_y.at[2 * slot + part],
            device_id=dev(rem(y + step + 4, 4) * 16 + z * 2 + core), device_id_type=MESH,
        )

    up_a, up_b = y_copy(1, 0, 0, snd, 0), y_copy(1, 0, 1, snd, 1)
    down_b, down_a = y_copy(-1, 2, 1, snd, 2), y_copy(-1, 2, 0, snd, 3)
    pass_a = y_copy(1, 1, 0, recv_y.at[0], 4)
    pass_b = y_copy(-1, 1, 1, recv_y.at[2], 5)
    for copy in (up_a, down_b, up_b, down_a):
        copy.start()

    zt[:, 256:384] = h3[...]
    zt[:, N:256] = e2[N:264, :] - dot(h3[...], e2[0:N, :])
    zt[:, 0:N] = e1[256:392, :] - dot(zt[:, N:384], e1[0:256, :])

    @pl.when(owner)
    def _():
        pltpu.make_async_remote_copy(
            src_ref=gath.at[pl.ds(0, 63)], dst_ref=gath.at[pl.ds(0, 63)], send_sem=s_n.at[0],
            recv_sem=r_n, device_id=dev(me + 1 - 2 * core), device_id_type=MESH,
        ).wait_recv()
        rhs = jnp.zeros((4, N), f32)
        for i in range(64):
            tile = gath[i]
            nsys[2 * i : 2 * i + 2, :] = tile[0:2, :]
            nlinks[2 * i : 2 * i + 2, :] = tile[2:4, :]
            rhs = rhs + tile[4:8, :]
        naug[0:N, :] = nlinks[...].T
        nvec[...] = rhs

    other = 2 * y + 1 - core
    acc_m[...] = snd[0:AUG, :] * snd[pl.ds(AUG + mine, 1), :]
    acc_o[...] = snd[0:AUG, :] * snd[pl.ds(AUG + other, 1), :]
    up_a.wait_recv()
    pass_a.start()
    down_b.wait_recv()
    pass_b.start()
    for slot, copies in ((0, (up_b,)), (2, (down_a,)), (1, (pass_a, pass_b))):
        for copy in copies:
            copy.wait_recv()
        acc_m[...] += recv_y[slot, 0:AUG, :] * recv_y[slot, pl.ds(AUG + mine, 1), :]
        acc_o[...] += recv_y[slot, 0:AUG, :] * recv_y[slot, pl.ds(AUG + other, 1), :]
    core_copy = pltpu.make_async_remote_copy(
        src_ref=acc_o, dst_ref=recv_c, send_sem=s_c, recv_sem=r_c,
        device_id=dev(me + 1 - 2 * core), device_id_type=MESH,
    )
    core_copy.start()
    core_copy.wait_recv()
    acc_m[...] += recv_c[...]

    def z_copy(source):
        return pltpu.make_async_remote_copy(
            src_ref=acc_m, dst_ref=recv_z.at[source], send_sem=s_z, recv_sem=r_z.at[source],
            device_id=dev(owner_leaf(mine, own_z)), device_id_type=MESH,
        )

    @pl.when(jnp.logical_not(owner))
    def _():
        z_copy(z).start()

    def slice_copy(src, dst, send_sem, recv_sem, t, by_group):
        if by_group:
            target = rem(grp + t, 8)
            device = {"leaf": owner_leaf(mine, 4 - div(target, 4)), "grp": target}
            slot = grp
            source = src
        else:
            target = rem(mine + t, 8)
            device = dev(owner_leaf(target, own_z))
            slot = mine
            source = src
        return pltpu.make_async_remote_copy(
            src_ref=source, dst_ref=dst.at[slot], send_sem=send_sem.at[t], recv_sem=recv_sem.at[slot],
            device_id=device, device_id_type=MESH,
        )

    def slot_wait(dst, send_sem, recv_sem, slot):
        pltpu.make_async_remote_copy(
            src_ref=dst.at[slot], dst_ref=dst.at[slot], send_sem=send_sem.at[0],
            recv_sem=recv_sem.at[slot], device_id=dev(me + 1 - 2 * core), device_id_type=MESH,
        ).wait_recv()

    def message(far, t):
        plane = far + (7 - 2 * far) * z_half
        target = rem(mine + t, 8)
        return pltpu.make_async_remote_copy(
            src_ref=msg, dst_ref=recv_n.at[mine], send_sem=s_m.at[far, t], recv_sem=r_m.at[mine],
            device_id=dev(div(target, 2) * 16 + plane * 2 + rem(target, 2)), device_id_type=MESH,
        )

    @pl.when(owner)
    def _():
        acc_m[N : N + 4, :] += -nvec[...]
        acc_m[0:N, :] += nsys[...]
        for t in (1, 7, 2, 6, 3, 5, 4):
            source = rem(own_z + t, 8)
            z_copy(source).wait_recv()
            acc_m[...] += recv_z[source]
        dinv[...] = acc_m[0:N, :]
        naug[N:AUG, :] = acc_m[N:AUG, :]
        invert(dinv, pbuf, qbuf)
        hmat[...] = dot(naug[...], dinv[...])
        rparts[...] = dot(hmat[...], nlinks[...])
        for q in range(8):
            send_r[q, 0:16, :] = rparts[16 * q : 16 * q + 16, :]
            send_r[q, 16:24, :] = rparts[N:AUG, :]

        for t in range(1, 8):
            slice_copy(send_r.at[rem(mine + t, 8)], recv_r, s_r, r_r, t, False).start()
        recv_r[mine] = send_r[mine]
        for t in range(1, 8):
            slot_wait(recv_r, s_r, r_r, rem(mine + t, 8))
        total = recv_r[0]
        for q in range(1, 8):
            total = total + recv_r[q]
        part[...] = total
        for t in range(1, 8):
            slice_copy(part, recv_g, s_g, r_g, t, True).start()
        recv_g[grp] = total
        for t in range(1, 8):
            slot_wait(recv_g, s_g, r_g, rem(grp + t, 8))
        total = recv_g[0]
        for q in range(1, 8):
            total = total + recv_g[q]
        tot[...] = total
        for t in range(1, 8):
            slice_copy(tot, recv_t, s_t, r_t, t, False).start()
        recv_t[mine] = total
        for t in range(1, 8):
            slot_wait(recv_t, s_t, r_t, rem(mine + t, 8))
        for q in range(8):
            dinv[16 * q : 16 * q + 16, :] = rmat[16 * q : 16 * q + 16, :] + recv_t[q, 0:16, :]
        invert(dinv, pbuf, qbuf)
        root_vec = row_bcast(rrhs[...]) - row_bcast(total[16:17, :])
        root = dot(root_vec, dinv[...])
        node = row_bcast(hmat[N : N + 1, :]) + dot(root, hmat[0:N, :])
        msg[0:1, :] = node[0:1, :]
        msg[1:2, :] = root[0:1, :]

        for far in (0, 1, 7, 2, 6, 3, 5, 4):
            def send(t, carry):
                message(far, t).start()
                return carry

            lax.fori_loop(1 if far == 4 else 0, 8, send, 0)
        recv_n[mine] = msg[...]

    @pl.when(owner)
    def _():
        for far in range(8):
            def drain(t, carry):
                message(far, t).wait_send()
                return carry

            lax.fori_loop(1 if far == 4 else 0, 8, drain, 0)

    for q in range(8):
        @pl.when(jnp.logical_or(jnp.logical_not(owner), mine != q))
        def _():
            slot_wait(recv_n, s_m, r_m, q)

    parent_dir = jnp.zeros((8, N), f32)
    for q in range(8):
        direction = row_bcast(recv_n[q, 0:1, :])
        parent_dir = parent_dir + direction * row_bcast(wts[q : q + 1, :])
        nd8[q : q + 1, :] = recv_n[q, 0:1, :]
    live = jnp.sum(wts[...], axis=0, keepdims=True)
    moved = dot(parent_dir, zt[0:N, :])
    for b in range(3):
        cols = slice(b * N, (b + 1) * N)
        packed[b : b + 1, :] = (zt[N : N + 1, cols] - moved[0:1, cols]) * live
    packed[3:4, :] = recv_n[0, 1:2, :]
    for a in range(2):
        values = lane_bcast(nd8[...], jnp.full((8, N), 2 * me + a, jnp.int32))
        packed[4 + a : 5 + a, :] = jnp.sum(jnp.where(sub == lane, values, 0.0), axis=0, keepdims=True)
    packed[6:8, :] = jnp.zeros((2, N), f32)

    for q in range(8):
        target = owner_leaf(q, own_z)

        @pl.when(target != me)
        def _():
            node_copy(q, target).wait_send()

    for copy in (up_a, up_b, down_a, down_b, pass_a, pass_b):
        copy.wait_send()
    core_copy.wait_send()

    @pl.when(jnp.logical_not(owner))
    def _():
        z_copy(z).wait_send()

    @pl.when(owner)
    def _():
        for t in range(1, 8):
            slice_copy(send_r.at[rem(mine + t, 8)], recv_r, s_r, r_r, t, False).wait_send()
            slice_copy(part, recv_g, s_g, r_g, t, True).wait_send()
            slice_copy(tot, recv_t, s_t, r_t, t, False).wait_send()


def unpack(packed, leaf_out, node_out, root_out):
    for b in range(3):
        leaf_out[:, b * N : (b + 1) * N] = packed[b : b + 1, :]
    node_out[...] = packed[4:6, 0:8]
    root_out[...] = packed[3:4, :]


def body(
    slot_parent, leaf_matrix, coupling, leaf_residual_rows, node_matrix, node_link, node_rhs,
    root_matrix, root_rhs,
):
    vmem = pl.BlockSpec(memory_space=pltpu.VMEM)
    buf = lambda *shape: pltpu.VMEM(shape, f32)
    dma = pltpu.SemaphoreType.DMA
    packed = pl.pallas_call(
        kernel,
        out_shape=jax.ShapeDtypeStruct((8, N), f32),
        in_specs=[
            pl.BlockSpec(memory_space=pltpu.SMEM), pl.BlockSpec(memory_space=pl.ANY),
            pl.BlockSpec(memory_space=pl.ANY),
        ] + [vmem] * 6,
        out_specs=vmem,
        scratch_shapes=[
            buf(384, 384), buf(384, N),
            buf(AUG, 384), buf(N, N), buf(N, N), buf(N, N), buf(64, N), buf(64, N), buf(64, N), buf(64, N),
            buf(392, N), buf(392, 256), buf(264, N), buf(AUG, N), buf(AUG, N), buf(8, N),
            buf(8, 8, N), buf(64, 8, N), buf(144, N), buf(3, 144, N), buf(AUG, N), buf(AUG, N),
            buf(AUG, N), buf(8, AUG, N),
            buf(N, N), buf(4, N), buf(N, N), buf(AUG, N), buf(AUG, N), buf(AUG, N), buf(8, 24, N),
            buf(8, 24, N), buf(24, N), buf(8, 24, N), buf(24, N), buf(8, 24, N),
            buf(2, N), buf(8, 2, N), buf(AUG, 384), buf(8, N),
            dma((3,)), dma((8,)), dma, dma((6,)), dma((6,)), dma, dma, dma, dma((8,)),
            dma((8,)), dma((8,)), dma((8,)), dma((8,)), dma((8,)), dma((8,)), dma((8, 8)), dma((8,)),
        ],
        compiler_params=pltpu.CompilerParams(collective_id=0, has_side_effects=True),
        name="newton_step",
    )(
        slot_parent, leaf_matrix, coupling, leaf_residual_rows, node_matrix, node_link, node_rhs.T,
        root_matrix, root_rhs[None, :],
    )
    leaf_dir, node_dir, root_dir = pl.pallas_call(
        unpack,
        out_shape=(
            jax.ShapeDtypeStruct((1, 384), f32),
            jax.ShapeDtypeStruct((2, 8), f32),
            jax.ShapeDtypeStruct((1, N), f32),
        ),
        in_specs=[vmem],
        out_specs=(vmem, vmem, vmem),
        name="unpack",
    )(packed)
    return leaf_dir, node_dir.T, root_dir[0]


def solution(mesh):
    return jax.shard_map(
        body,
        mesh=mesh,
        in_specs=(
            P(("leaf", "grp")),
            P(("leaf", "grp"), None, None),
            P(("leaf", "grp"), None, None),
            P(("leaf", "grp"), None),
            P("grp", "leaf", None),
            P("grp", "leaf", None),
            P("grp", "leaf"),
            P(),
            P(),
        ),
        out_specs=(P(("leaf", "grp"), None), P("grp", "leaf"), P()),
        check_vma=False,
    )
```

```python
import jax
import jax.numpy as jnp
from jax import lax
from jax.experimental import pallas as pl
from jax.experimental.pallas import tpu as pltpu
from jax.sharding import PartitionSpec as P

f32 = jnp.float32
MESH = pl.DeviceIdType.MESH
HI = lax.Precision.HIGHEST
N = 128
AUG = 136
PANEL = 64
GROUPS = PANEL // 8


def rem(a, b):
    return a % b if isinstance(a, int) else lax.rem(a, b)


def div(a, b):
    return a // b if isinstance(a, int) else lax.div(a, b)


def dot(a, b):
    return jnp.dot(a, b, precision=HI, preferred_element_type=f32)


def dot_nt(a, b):
    return lax.dot_general(
        a, b, (((1,), (1,)), ((), ())), precision=HI, preferred_element_type=f32
    )


def lane_bcast(x, index):
    dims = lax.GatherDimensionNumbers(
        offset_dims=(), collapsed_slice_dims=(1,), start_index_map=(1,),
        operand_batching_dims=(0,), start_indices_batching_dims=(0,),
    )
    return lax.gather(
        x, index[:, :, None], dims, (1, 1), mode=lax.GatherScatterMode.PROMISE_IN_BOUNDS
    )


def row_bcast(row):
    return jnp.broadcast_to(row, (8, N))


def invert(d_ref, p_ref, q_ref):
    lane = lax.broadcasted_iota(jnp.int32, (8, N), 1)
    sub = lax.broadcasted_iota(jnp.int32, (8, N), 0)
    for h in range(N // PANEL):
        top = h * PANEL
        first = d_ref[top : top + 8, :]
        for j in range(8):
            p_ref[8 * j : 8 * j + 8, :] = lane_bcast(first, jnp.full((8, N), top + j, jnp.int32))

        for k in range(GROUPS):
            base = top + k * 8
            base_next = top + min(k + 1, GROUPS - 1) * 8
            here = [jnp.full((8, N), base + j, jnp.int32) for j in range(8)]
            after = [jnp.full((8, N), base_next + j, jnp.int32) for j in range(8)]
            s = {}
            for j in range(8):
                for i in range(j + 1):
                    s[i, j] = row_bcast(p_ref[8 * j + i : 8 * j + i + 1, :])
            r = [row_bcast(d_ref[pl.ds(base + j, 1), :]) for j in range(8)]
            d = [d_ref[top + g * 8 : top + (g + 1) * 8, :] for g in range(GROUPS)]
            dn = d_ref[pl.ds(base_next, 8), :]
            cn, pn, c = [], [], []
            for j in range(8):
                cn.append(lane_bcast(dn, here[j]))
            for j in range(8):
                pn.append(lane_bcast(dn, after[j]))
            for j in range(8):
                c.append([lane_bcast(d[g], here[j]) for g in range(GROUPS)])
            inside = (lane >= base) & (lane < base + 8)
            r = [jnp.where(inside, jnp.where(lane == base + j, 1.0, 0.0), r[j]) for j in range(8)]
            low, inv = {}, []
            for j in range(8):
                inv.append(1.0 / s[j, j])
                for i in range(j + 1, 8):
                    low[i, j] = s[j, i] * inv[j]
                for i in range(j + 1, 8):
                    for m in range(i, 8):
                        s[i, m] = s[i, m] - low[i, j] * s[j, m]
                q_ref[8 * j : 8 * j + 8, :] = cn[j]
                scaled = cn[j] * inv[j]
                for i in range(8):
                    pn[i] = pn[i] - scaled * row_bcast(q_ref[8 * j + i : 8 * j + i + 1, :])
                for i in range(j + 1, 8):
                    cn[i] = cn[i] - low[i, j] * cn[j]
                for i in range(j + 1, 8):
                    r[i] = r[i] - low[i, j] * r[j]
            for j in range(8):
                p_ref[8 * j : 8 * j + 8, :] = pn[j]
            x = [r[j] * inv[j] for j in range(8)]
            for j in range(7, -1, -1):
                for i in range(j):
                    x[i] = x[i] - low[j, i] * x[j]
            for g in range(GROUPS):
                kept = jnp.where(inside, 0.0, d[g])
                t = [c[j][g] * x[j] for j in range(8)]
                d_ref[top + g * 8 : top + (g + 1) * 8, :] = kept - (
                    ((t[0] + t[1]) + (t[2] + t[3])) + ((t[4] + t[5]) + (t[6] + t[7]))
                )
            new = x[0]
            for j in range(1, 8):
                new = jnp.where(sub == j, x[j], new)
            d_ref[pl.ds(base, 8), :] = new
        pan = d_ref[top : top + PANEL, :]
        wide = lax.broadcasted_iota(jnp.int32, (N - PANEL, N), 1)
        in_pan = (wide >= top) & (wide < top + PANEL)
        if top == 0:
            rest = d_ref[PANEL:N, :]
        elif top + PANEL == N:
            rest = d_ref[0:top, :]
        else:
            rest = jnp.concatenate([d_ref[0:top, :], d_ref[top + PANEL : N, :]], axis=0)
        out = jnp.where(in_pan, 0.0, rest) - dot(rest[:, top : top + PANEL], pan)
        if top > 0:
            d_ref[0:top, :] = out[0:top, :]
        if top + PANEL < N:
            d_ref[top + PANEL : N, :] = out[top : N - PANEL, :]


def kernel(
    parent, amat, coup, resid, nmat, nlink, nrhs, rmat, rrhs,
    packed,
    av, cv, bt, dinv, dinv2, dinv3, pbuf, qbuf, pbuf2, qbuf2, e1, rem1, e2, rem2, h3, wts,
    ntile, gath, snd, recv_y, acc_o, recv_c, acc_m, recv_z,
    nsys, nvec, nlinks, naug, hmat, rparts, send_r, recv_r, part, recv_g, tot, recv_t,
    msg, recv_n, zt, nd8,
    s_l, s_n, r_n, s_y, r_y, s_c, r_c, s_z, r_z, s_r, r_r, s_g, r_g, s_t, r_t, s_m, r_m,
):
    me = lax.axis_index("leaf")
    grp = lax.axis_index("grp")
    y, z, core = div(me, 16), rem(div(me, 2), 8), rem(me, 2)
    z_half = div(grp, 4)
    own_z = 4 - 2 * z_half
    owner = z == own_z
    mine = 2 * y + core

    def dev(leaf):
        return {"leaf": leaf, "grp": grp}

    def owner_leaf(m, oz):
        return div(m, 2) * 16 + oz * 2 + rem(m, 2)

    local = [
        pltpu.make_async_copy(amat.at[0, pl.ds(0, N), pl.ds(0, N)], dinv, s_l.at[0]),
        pltpu.make_async_copy(amat.at[0], av, s_l.at[1]),
        pltpu.make_async_copy(coup.at[0], cv, s_l.at[2]),
    ]
    for copy in local:
        copy.start()

    barrier = pltpu.get_barrier_semaphore()

    def greet(leaf):
        pl.semaphore_signal(barrier, inc=1, device_id=dev(leaf), device_id_type=MESH)

    @pl.when(jnp.logical_not(owner))
    def _():
        for step in (1, 3):
            greet(rem(y + step, 4) * 16 + z * 2 + core)
        greet(me + 1 - 2 * core)
        for q in range(8):
            greet(owner_leaf(q, own_z))

    @pl.when(owner)
    def _():
        def greet_all(t, carry):
            greet(rem(me + t, 64))
            return carry

        lax.fori_loop(1, 64, greet_all, 0)

        def greet_far(t, carry):
            g = rem(grp + t, 8)
            pl.semaphore_signal(
                barrier, inc=1,
                device_id={"leaf": owner_leaf(mine, 4 - 2 * div(g, 4)), "grp": g}, device_id_type=MESH,
            )
            return carry

        lax.fori_loop(1, 8, greet_far, 0)

    local[0].wait()
    invert(dinv, pbuf, qbuf)

    sub = lax.broadcasted_iota(jnp.int32, (8, N), 0)
    lane = lax.broadcasted_iota(jnp.int32, (8, N), 1)
    sub4 = lax.broadcasted_iota(jnp.int32, (4, N), 0)
    lane4 = lax.broadcasted_iota(jnp.int32, (4, N), 1)
    wts[...] = jnp.where(sub == parent[0], 1.0, 0.0)
    nd8[...] = jnp.zeros((8, N), f32)
    nd8[0:2, 0:8] = nrhs[...]
    pair = nd8[...]
    for q in range(8):
        value = lane_bcast(pair, jnp.full((8, N), q, jnp.int32))
        ntile[q, 0:2, :] = nmat[q]
        ntile[q, 2:4, :] = nlink[q]
        ntile[q, 4:8, :] = jnp.where(
            sub4 == 0,
            jnp.where(lane4 == 2 * me, value[0:1, :], 0.0)
            + jnp.where(lane4 == 2 * me + 1, value[1:2, :], 0.0),
            0.0,
        )

    @pl.when(owner)
    def _():
        pl.semaphore_wait(barrier, 70)

    @pl.when(jnp.logical_not(owner))
    def _():
        pl.semaphore_wait(barrier, 11)

    def node_copy(q, target):
        return pltpu.make_async_remote_copy(
            src_ref=ntile.at[q], dst_ref=gath.at[me], send_sem=s_n.at[q], recv_sem=r_n,
            device_id=dev(target), device_id_type=MESH,
        )

    for q in range(8):
        target = owner_leaf(q, own_z)

        @pl.when(target != me)
        def _():
            node_copy(q, target).start()

        @pl.when(target == me)
        def _():
            gath[me] = ntile[q]

    local[1].wait()
    local[2].wait()
    for b in range(3):
        bt[0:N, b * N : (b + 1) * N] = cv[b * N : (b + 1) * N, :].T
        bt[N:AUG, b * N : (b + 1) * N] = jnp.where(
            sub == 0, row_bcast(resid[:, b * N : (b + 1) * N]), 0.0
        )
    e1[0:N, :] = dot(av[N:256, 0:N], dinv[...])
    dinv2[...] = av[N:256, N:256] - dot(e1[0:N, :], av[0:N, N:256])
    e1[N:392, :] = dot(jnp.concatenate([av[256:384, 0:N], bt[:, 0:N]], axis=0), dinv[...])
    rem1[0:N, N:256] = av[N:256, 256:384] - dot(e1[0:N, :], av[0:N, 256:384])
    rem1[N:256, :] = av[256:384, N:384] - dot(e1[N:256, :], av[0:N, N:384])
    rem1[256:392, :] = bt[:, N:384] - dot(e1[256:392, :], av[0:N, N:384])
    snd[0:AUG, :] = dot_nt(e1[256:392, :], bt[0:N, 0:N])
    invert(dinv2, pbuf2, qbuf2)
    e2[0:N, :] = dot(rem1[N:256, 0:N], dinv2[...])
    dinv3[...] = rem1[N:256, N:256] - dot(e2[0:N, :], rem1[0:N, N:256])
    e2[N:264, :] = dot(rem1[256:392, 0:N], dinv2[...])
    rem2[...] = rem1[256:392, N:256] - dot(e2[N:264, :], rem1[0:N, N:256])
    snd[0:AUG, :] += dot_nt(e2[N:264, :], rem1[256:384, 0:N])
    invert(dinv3, pbuf, qbuf)
    h3[...] = dot(rem2[...], dinv3[...])
    snd[0:AUG, :] += dot_nt(h3[...], rem2[0:N, :])
    snd[AUG : AUG + 8, :] = wts[...]

    def y_copy(step, slot, part, src, sem):
        rows = pl.ds(72 * part, 72)
        return pltpu.make_async_remote_copy(
            src_ref=src.at[rows], dst_ref=recv_y.at[slot, rows], send_sem=s_y.at[sem],
            recv_sem=r_y.at[2 * slot + part],
            device_id=dev(rem(y + step + 4, 4) * 16 + z * 2 + core), device_id_type=MESH,
        )

    up_a, up_b = y_copy(1, 0, 0, snd, 0), y_copy(1, 0, 1, snd, 1)
    down_b, down_a = y_copy(-1, 2, 1, snd, 2), y_copy(-1, 2, 0, snd, 3)
    pass_a = y_copy(1, 1, 0, recv_y.at[0], 4)
    pass_b = y_copy(-1, 1, 1, recv_y.at[2], 5)
    for copy in (up_a, down_b, up_b, down_a):
        copy.start()

    zt[:, 256:384] = h3[...]
    zt[:, N:256] = e2[N:264, :] - dot(h3[...], e2[0:N, :])
    zt[:, 0:N] = e1[256:392, :] - dot(zt[:, N:384], e1[0:256, :])

    @pl.when(owner)
    def _():
        pltpu.make_async_remote_copy(
            src_ref=gath.at[pl.ds(0, 63)], dst_ref=gath.at[pl.ds(0, 63)], send_sem=s_n.at[0],
            recv_sem=r_n, device_id=dev(me + 1 - 2 * core), device_id_type=MESH,
        ).wait_recv()
        rhs = jnp.zeros((4, N), f32)
        for i in range(64):
            tile = gath[i]
            nsys[2 * i : 2 * i + 2, :] = tile[0:2, :]
            nlinks[2 * i : 2 * i + 2, :] = tile[2:4, :]
            rhs = rhs + tile[4:8, :]
        naug[0:N, :] = nlinks[...].T
        nvec[...] = rhs

    other = 2 * y + 1 - core
    acc_m[...] = snd[0:AUG, :] * snd[pl.ds(AUG + mine, 1), :]
    acc_o[...] = snd[0:AUG, :] * snd[pl.ds(AUG + other, 1), :]
    up_a.wait_recv()
    pass_a.start()
    down_b.wait_recv()
    pass_b.start()
    for slot, copies in ((0, (up_b,)), (2, (down_a,)), (1, (pass_a, pass_b))):
        for copy in copies:
            copy.wait_recv()
        acc_m[...] += recv_y[slot, 0:AUG, :] * recv_y[slot, pl.ds(AUG + mine, 1), :]
        acc_o[...] += recv_y[slot, 0:AUG, :] * recv_y[slot, pl.ds(AUG + other, 1), :]
    core_copy = pltpu.make_async_remote_copy(
        src_ref=acc_o, dst_ref=recv_c, send_sem=s_c, recv_sem=r_c,
        device_id=dev(me + 1 - 2 * core), device_id_type=MESH,
    )
    core_copy.start()
    core_copy.wait_recv()
    acc_m[...] += recv_c[...]

    def z_copy(source):
        return pltpu.make_async_remote_copy(
            src_ref=acc_m, dst_ref=recv_z.at[source], send_sem=s_z, recv_sem=r_z.at[source],
            device_id=dev(owner_leaf(mine, own_z)), device_id_type=MESH,
        )

    @pl.when(jnp.logical_not(owner))
    def _():
        z_copy(z).start()

    def slice_copy(src, dst, send_sem, recv_sem, t, by_group):
        if by_group:
            target = rem(grp + t, 8)
            device = {"leaf": owner_leaf(mine, 4 - 2 * div(target, 4)), "grp": target}
            slot = grp
            source = src
        else:
            target = rem(mine + t, 8)
            device = dev(owner_leaf(target, own_z))
            slot = mine
            source = src
        return pltpu.make_async_remote_copy(
            src_ref=source, dst_ref=dst.at[slot], send_sem=send_sem.at[t], recv_sem=recv_sem.at[slot],
            device_id=device, device_id_type=MESH,
        )

    def slot_wait(dst, send_sem, recv_sem, slot):
        pltpu.make_async_remote_copy(
            src_ref=dst.at[slot], dst_ref=dst.at[slot], send_sem=send_sem.at[0],
            recv_sem=recv_sem.at[slot], device_id=dev(me + 1 - 2 * core), device_id_type=MESH,
        ).wait_recv()

    def message(far, t):
        plane = far + ((14 - far) % 8 - far) * z_half
        target = rem(mine + t, 8)
        return pltpu.make_async_remote_copy(
            src_ref=msg, dst_ref=recv_n.at[mine], send_sem=s_m.at[far, t], recv_sem=r_m.at[mine],
            device_id=dev(div(target, 2) * 16 + plane * 2 + rem(target, 2)), device_id_type=MESH,
        )

    @pl.when(owner)
    def _():
        acc_m[N : N + 4, :] += -nvec[...]
        acc_m[0:N, :] += nsys[...]
        for t in (1, 7, 2, 6, 3, 5, 4):
            source = rem(own_z + t, 8)
            z_copy(source).wait_recv()
            acc_m[...] += recv_z[source]
        dinv[...] = acc_m[0:N, :]
        naug[N:AUG, :] = acc_m[N:AUG, :]
        invert(dinv, pbuf, qbuf)
        hmat[...] = dot(naug[...], dinv[...])
        rparts[...] = dot(hmat[...], nlinks[...])
        for q in range(8):
            send_r[q, 0:16, :] = rparts[16 * q : 16 * q + 16, :]
            send_r[q, 16:24, :] = rparts[N:AUG, :]

        for t in range(1, 8):
            slice_copy(send_r.at[rem(mine + t, 8)], recv_r, s_r, r_r, t, False).start()
        recv_r[mine] = send_r[mine]
        for t in range(1, 8):
            slot_wait(recv_r, s_r, r_r, rem(mine + t, 8))
        total = recv_r[0]
        for q in range(1, 8):
            total = total + recv_r[q]
        part[...] = total
        for t in range(1, 8):
            slice_copy(part, recv_g, s_g, r_g, t, True).start()
        recv_g[grp] = total
        for t in range(1, 8):
            slot_wait(recv_g, s_g, r_g, rem(grp + t, 8))
        total = recv_g[0]
        for q in range(1, 8):
            total = total + recv_g[q]
        tot[...] = total[0:16, :]
        for t in range(1, 8):
            slice_copy(tot, recv_t, s_t, r_t, t, False).start()
        recv_t[mine] = total[0:16, :]
        for t in range(1, 8):
            slot_wait(recv_t, s_t, r_t, rem(mine + t, 8))
        for q in range(8):
            dinv[16 * q : 16 * q + 16, :] = rmat[16 * q : 16 * q + 16, :] + recv_t[q, 0:16, :]
        invert(dinv, pbuf, qbuf)
        root_vec = row_bcast(rrhs[...]) - row_bcast(total[16:17, :])
        root = dot(root_vec, dinv[...])
        node = row_bcast(hmat[N : N + 1, :]) + dot(root, hmat[0:N, :])
        msg[0:1, :] = node[0:1, :]
        msg[1:2, :] = root[0:1, :]

        for far in (0, 1, 7, 2, 6, 3, 5, 4):
            def send(t, carry):
                message(far, t).start()
                return carry

            lax.fori_loop(1 if far == 4 else 0, 8, send, 0)
        recv_n[mine] = msg[...]

    @pl.when(owner)
    def _():
        for far in range(8):
            def drain(t, carry):
                message(far, t).wait_send()
                return carry

            lax.fori_loop(1 if far == 4 else 0, 8, drain, 0)

    for q in range(8):
        @pl.when(jnp.logical_or(jnp.logical_not(owner), mine != q))
        def _():
            slot_wait(recv_n, s_m, r_m, q)

    parent_dir = jnp.zeros((8, N), f32)
    for q in range(8):
        direction = row_bcast(recv_n[q, 0:1, :])
        parent_dir = parent_dir + direction * row_bcast(wts[q : q + 1, :])
        nd8[q : q + 1, :] = recv_n[q, 0:1, :]
    live = jnp.sum(wts[...], axis=0, keepdims=True)
    moved = dot(parent_dir, zt[0:N, :])
    for b in range(3):
        cols = slice(b * N, (b + 1) * N)
        packed[b : b + 1, :] = (zt[N : N + 1, cols] - moved[0:1, cols]) * live
    packed[3:4, :] = recv_n[0, 1:2, :]
    for a in range(2):
        values = lane_bcast(nd8[...], jnp.full((8, N), 2 * me + a, jnp.int32))
        packed[4 + a : 5 + a, :] = jnp.sum(jnp.where(sub == lane, values, 0.0), axis=0, keepdims=True)
    packed[6:8, :] = jnp.zeros((2, N), f32)

    for q in range(8):
        target = owner_leaf(q, own_z)

        @pl.when(target != me)
        def _():
            node_copy(q, target).wait_send()

    for copy in (up_a, up_b, down_a, down_b, pass_a, pass_b):
        copy.wait_send()
    core_copy.wait_send()

    @pl.when(jnp.logical_not(owner))
    def _():
        z_copy(z).wait_send()

    @pl.when(owner)
    def _():
        for t in range(1, 8):
            slice_copy(send_r.at[rem(mine + t, 8)], recv_r, s_r, r_r, t, False).wait_send()
            slice_copy(part, recv_g, s_g, r_g, t, True).wait_send()
            slice_copy(tot, recv_t, s_t, r_t, t, False).wait_send()


def unpack(packed, leaf_out, node_out, root_out):
    for b in range(3):
        leaf_out[:, b * N : (b + 1) * N] = packed[b : b + 1, :]
    node_out[...] = packed[4:6, 0:8]
    root_out[...] = packed[3:4, :]


def body(
    slot_parent, leaf_matrix, coupling, leaf_residual_rows, node_matrix, node_link, node_rhs,
    root_matrix, root_rhs,
):
    vmem = pl.BlockSpec(memory_space=pltpu.VMEM)
    buf = lambda *shape: pltpu.VMEM(shape, f32)
    dma = pltpu.SemaphoreType.DMA
    packed = pl.pallas_call(
        kernel,
        out_shape=jax.ShapeDtypeStruct((8, N), f32),
        in_specs=[
            pl.BlockSpec(memory_space=pltpu.SMEM), pl.BlockSpec(memory_space=pl.ANY),
            pl.BlockSpec(memory_space=pl.ANY),
        ] + [vmem] * 6,
        out_specs=vmem,
        scratch_shapes=[
            buf(384, 384), buf(384, N),
            buf(AUG, 384), buf(N, N), buf(N, N), buf(N, N), buf(64, N), buf(64, N), buf(64, N), buf(64, N),
            buf(392, N), buf(392, 256), buf(264, N), buf(AUG, N), buf(AUG, N), buf(8, N),
            buf(8, 8, N), buf(64, 8, N), buf(144, N), buf(3, 144, N), buf(AUG, N), buf(AUG, N),
            buf(AUG, N), buf(8, AUG, N),
            buf(N, N), buf(4, N), buf(N, N), buf(AUG, N), buf(AUG, N), buf(AUG, N), buf(8, 24, N),
            buf(8, 24, N), buf(24, N), buf(8, 24, N), buf(16, N), buf(8, 16, N),
            buf(2, N), buf(8, 2, N), buf(AUG, 384), buf(8, N),
            dma((3,)), dma((8,)), dma, dma((6,)), dma((6,)), dma, dma, dma, dma((8,)),
            dma((8,)), dma((8,)), dma((8,)), dma((8,)), dma((8,)), dma((8,)), dma((8, 8)), dma((8,)),
        ],
        compiler_params=pltpu.CompilerParams(collective_id=0, has_side_effects=True),
        name="newton_step",
    )(
        slot_parent, leaf_matrix, coupling, leaf_residual_rows, node_matrix, node_link, node_rhs.T,
        root_matrix, root_rhs[None, :],
    )
    leaf_dir, node_dir, root_dir = pl.pallas_call(
        unpack,
        out_shape=(
            jax.ShapeDtypeStruct((1, 384), f32),
            jax.ShapeDtypeStruct((2, 8), f32),
            jax.ShapeDtypeStruct((1, N), f32),
        ),
        in_specs=[vmem],
        out_specs=(vmem, vmem, vmem),
        name="unpack",
    )(packed)
    return leaf_dir, node_dir.T, root_dir[0]


def solution(mesh):
    return jax.shard_map(
        body,
        mesh=mesh,
        in_specs=(
            P(("leaf", "grp")),
            P(("leaf", "grp"), None, None),
            P(("leaf", "grp"), None, None),
            P(("leaf", "grp"), None),
            P("grp", "leaf", None),
            P("grp", "leaf", None),
            P("grp", "leaf"),
            P(),
            P(),
        ),
        out_specs=(P(("leaf", "grp"), None), P("grp", "leaf"), P()),
        check_vma=False,
    )
```
